32 devices in a mesh: dp: 2 (over x), ep: 16 (over z, y, core).
Axes of the slice: x: 2, y: 2, z: 4, core: 2. Of those that a mesh axis runs over, the one named last changes fastest.
Arguments:
- queries: bfloat16 [2048, 36864], P('ep', 'dp'), may hold values from -40 to 40
- suffix_latent: bfloat16 [2048, 576], P('ep'), may hold values from -10 to 10
- page_pool: bfloat16 [128, 36864], P('ep'), may hold values from -6 to 6
- page_owner: int32 [16, 32], P('ep'), may hold values from 0 to 15, as said below
- page_slot: int32 [16, 32], P('ep'), may hold values from 0 to 7
- prefix_len: int32 [16], P('ep'), may hold values from 1025 to 2048, as said below
- moe_input: bfloat16 [512, 3584], P(('dp', 'ep')), may hold values from -6 to 6
- expert_ids: int32 [512, 8], P(('dp', 'ep')), may hold values from 0 to 15, all different within a row; in each aligned block of 16 rows (0 to 15, 16 to 31, ...) at most 10 rows name the same one
- gate_weights: float32 [512, 8], P(('dp', 'ep')), may hold values from 0.1 to 0.6
- w_gate: bfloat16 [16, 3584, 1024], P('ep', None, 'dp'), may hold values from -0.09375 to 0.09375
- w_up: bfloat16 [16, 3584, 1024], P('ep', None, 'dp'), may hold values from -0.09375 to 0.09375
- w_down: bfloat16 [16, 1024, 3584], P('ep', 'dp'), may hold values from -0.1875 to 0.1875
Outputs:
- attn_context: bfloat16 [2048, 32768], P('ep', 'dp')
- moe_output: bfloat16 [512, 3584], P(('dp', 'ep'))
The draws below stay inside these ranges and needn't reach their ends.
Inputs may be any that keep to these rules, and one draw needn't show every extreme that they name: `page_owner`: for a multiple m of the ep axis's size, the pages m, m + 1, ... of one request up to m + that size - 1 have distinct owners, so page k is the (k div that size)-th page of its request on its owner; entries past a request's prefix are valid page references too. `prefix_len`: some request has the longest prefix, 2048 tokens. `expert_ids`: in the 16 rows of one device no expert is named by more than 10 rows.
All inputs are finite; a program needn't handle non-finite values.
Results may differ from the reference program's by a relative error of at most 0.0057.
Values may be sent and summed in bfloat16 or wider, within the bound.
No kernel may reach another device: no remote copies, remote signals or barrier semaphores. Data moves between devices by JAX's collectives and lax.ppermute only.
A program may use at most 192 MiB of HBM per device.

```python
import math
import jax
import jax.numpy as jnp
import numpy as np
from jax import lax

LATENT = 512
ROPE = 64
TOP = 8
HID = 3584
FFN = 1024
HEADS = 64
PAGE = 64
PMAX = 32
PAGES_DEV = 8
TQ = 128
TM = 16
EXPERTS = 16
CAP = 10
KD = 576
REQS = 16
TOK_A = 2048
TOK_M = 512
N_EP = 16


def joint_attention(key):
    tokens = TQ * REQS
    key_width = LATENT + ROPE
    subkeys = jax.random.split(jax.random.fold_in(key, 7301), 2)
    suffix = jax.random.normal(subkeys[0], (tokens, key_width), jnp.float32)
    queries = jax.random.normal(subkeys[1], (tokens, HEADS, key_width), jnp.float32)
    return (queries.reshape(tokens, HEADS * key_width), suffix)


def draw_queries(key, part):
    return joint_attention(key)[0].astype(jnp.bfloat16)


def draw_suffix_latent(key, part):
    return joint_attention(key)[1].astype(jnp.bfloat16)


def draw_page_owner(key, part):
    request_keys = jax.random.split(jax.random.fold_in(key, 4409), REQS)
    permuted = jax.vmap(lambda single: jax.random.permutation(single, N_EP))(request_keys).astype(jnp.int32)
    column = jnp.arange(PMAX, dtype=jnp.int32) % N_EP
    return permuted[:, column]


def draw_prefix_len(key, part):
    subkeys = jax.random.split(jax.random.fold_in(key, 9127), 2)
    longest = PMAX * PAGE
    lengths = jax.random.randint(subkeys[0], (REQS,), longest // 2 + 1, longest + 1)
    picked = jax.random.randint(subkeys[1], (), 0, REQS)
    filled = jnp.arange(REQS, dtype=jnp.int32) == picked
    return jnp.where(filled, longest, lengths).astype(jnp.int32)


def with_ends(values, rng, smallest, high):
    dims = values.shape
    index_at = [jax.random.randint(jax.random.fold_in(rng, axis), (), 0, dims[axis]) for axis in range(len(dims))]
    values = values.at[tuple(index_at)].set(smallest)
    longest = dims.index(max(dims))
    index_at[longest] = (index_at[longest] + 1) % dims[longest]
    return values.at[tuple(index_at)].set(high)


def shard_levels(own_key, extent, cuts, smallest, largest):
    gain = 1.0
    for dim, shards_of in cuts:
        heights = jax.random.uniform(jax.random.fold_in(jax.random.fold_in(own_key, 6), dim), (shards_of,), jnp.float32, smallest / len(cuts), largest / len(cuts))
        gain = gain * jnp.repeat(jnp.exp(heights), extent[dim] // shards_of).reshape((-1,) + (1,) * (len(extent) - 1 - dim))
    return gain


def shared_out(key, own, number, rows, amount, top, limit, slope):
    sequence = jax.random.permutation(key, amount)
    packed, ordinary = load_shares(amount, rows * top, limit, slope, True), load_shares(amount, rows * top, limit, slope, False)
    places = jnp.arange(amount)

    def named(sizes, turn):
        used = int((sizes > 0).sum())
        fixed = max(1, used // 4)
        passed = fixed + (places - fixed + turn * (used - fixed)) % max(1, amount - fixed)
        return jnp.zeros((amount,), jnp.int32).at[sequence[jnp.where(places < fixed, places, passed)]].set(jnp.asarray(sizes, jnp.int32))

    sizes = jnp.where(number % 4 == 0, named(packed, number // 4), named(ordinary, number - number // 4 - 1))
    mixed = jax.random.permutation(jax.random.fold_in(own, 3), amount)
    giver, taker = mixed[0:amount // 2 * 2:2], mixed[1:amount // 2 * 2:2]
    slack = jnp.minimum(sizes[giver] - 1, limit - sizes[taker]) // 2
    slack = jnp.where((giver == sequence[0]) | (taker == sequence[0]) | (sizes[taker] == 0), 0, jnp.maximum(slack, 0))
    passed = jax.random.randint(jax.random.fold_in(own, 4), (amount // 2,), 0, 1 << 20) % (slack + 1)
    sizes = sizes.at[giver].add(-passed).at[taker].add(passed)
    items = jnp.searchsorted(jnp.cumsum(sizes), jnp.arange(rows * top), side="right").astype(jnp.int32)
    grid = items.reshape(top, rows).T
    grid = grid[jax.random.permutation(jax.random.fold_in(own, 1), rows)]
    turn = jax.random.randint(jax.random.fold_in(own, 2), (rows, 1), 0, top)
    return jnp.take_along_axis(grid, (jnp.arange(top)[None, :] + turn) % top, axis=1)


def load_shares(number_of, total, reach, skew, full):
    loads = [(1 << 20) // math.isqrt(standing ** skew) + 1 for standing in range(1, number_of + 1)]
    largest = reach if full else min(reach, max(-(-total // number_of), total * loads[0] // sum(loads)))
    least = 1 if total - largest >= number_of - 1 else 0
    given, spare = [largest] + [least] * (number_of - 1), total - largest - least * (number_of - 1)
    while spare > 0:
        free = [i for i in range(1, number_of) if given[i] < largest] or [i for i in range(1, number_of) if given[i] < reach]
        pool, remaining = sum([loads[i] for i in free]), spare
        for i in free:
            more = min(reach - given[i], max(1, remaining * loads[i] // pool), spare)
            given[i] = given[i] + more
            spare = spare - more
    return np.array(given)


def normal_values(rng, shape, scale, bound, shards=(), held_as=jnp.bfloat16):
    level = shard_levels(rng, shape, shards, -0.22, 0.18) if shards else 1.0
    drawn = jax.random.normal(rng, shape, jnp.float32) * scale * level
    return jnp.minimum(jnp.maximum(drawn, -bound), bound).astype(held_as)


def setup_inputs(seed: int = 0) -> dict:
    seeds = jax.random.split(jax.random.key(seed), 13)
    queries = draw_queries(jax.random.fold_in(seeds[12], 71), 0)
    suffix_latent = draw_suffix_latent(jax.random.fold_in(seeds[12], 71), 0)
    page_pool = normal_values(seeds[2], (REQS * PAGES_DEV, PAGE * KD), 1.0, 6.0, ((0, 16),))
    page_owner = draw_page_owner(jax.random.fold_in(seeds[12], 71), 0)
    page_slot = with_ends(jax.random.randint(seeds[4], (REQS, PMAX), 0, PAGES_DEV), jax.random.fold_in(seeds[4], 1), 0, PAGES_DEV - 1).astype(jnp.int32)
    prefix_len = draw_prefix_len(jax.random.fold_in(seeds[12], 71), 0)
    moe_input = normal_values(seeds[6], (TOK_M, HID), 1.0, 6.0, ((0, 32),))
    expert_ids_keys = jax.random.split(jax.random.fold_in(seeds[7], 1), TOK_M // TM)
    expert_ids_turns = jax.random.permutation(jax.random.fold_in(seeds[7], 3), TOK_M // TM)
    expert_ids = jax.vmap(lambda own, number: shared_out(jax.random.fold_in(seeds[7], 2), own, number, TM, EXPERTS, TOP, CAP, 2))(expert_ids_keys, expert_ids_turns).reshape((TOK_M, TOP))
    gate_weights = jnp.clip(0.1 + 0.5 * jax.random.uniform(seeds[8], (TOK_M, TOP), jnp.float32) ** shard_levels(seeds[8], (TOK_M, TOP), ((0, 32),), -0.2, 0.2), 0.1, 0.6)
    w_gate = normal_values(seeds[9], (EXPERTS, HID, FFN), HID ** -0.5, 0.09375, ((0, 16), (2, 2)))
    w_up = normal_values(seeds[10], (EXPERTS, HID, FFN), HID ** -0.5, 0.09375, ((0, 16), (2, 2)))
    w_down = normal_values(seeds[11], (EXPERTS, FFN, HID), FFN ** -0.5, 0.1875, ((0, 16), (1, 2)))
    return dict(queries=queries, suffix_latent=suffix_latent, page_pool=page_pool, page_owner=page_owner, page_slot=page_slot, prefix_len=prefix_len, moe_input=moe_input, expert_ids=expert_ids, gate_weights=gate_weights, w_gate=w_gate, w_up=w_up, w_down=w_down)


score_scale = 0.07216878364870322
neg_large = -1.0e30


def attend(query_rows, suffix_rows, prefix_keys, length):
    new_tokens = suffix_rows.shape[0]
    key_width = suffix_rows.shape[1]
    head_count = query_rows.shape[1] // key_width
    flat_queries = query_rows.reshape(new_tokens * head_count, key_width)
    all_keys = jnp.concatenate([prefix_keys, suffix_rows], axis=0)
    scores = lax.dot_general(flat_queries, all_keys, (((1,), (1,)), ((), ())), preferred_element_type=jnp.float32) * score_scale
    prefix_count = prefix_keys.shape[0]
    key_index = jnp.arange(prefix_count + new_tokens, dtype=jnp.int32)[None, :]
    row_token = (jnp.arange(new_tokens * head_count, dtype=jnp.int32) // head_count)[:, None]
    allowed = jnp.where(key_index < prefix_count, key_index < length, key_index - prefix_count <= row_token)
    masked = jnp.where(allowed, scores, neg_large)
    row_max = jnp.max(masked, axis=1, keepdims=True)
    exponent = jnp.where(allowed, jnp.exp(masked - row_max), 0.0)
    probs = (exponent / jnp.sum(exponent, axis=1, keepdims=True)).astype(jnp.bfloat16)
    context = jnp.dot(probs, all_keys[:, :LATENT], preferred_element_type=jnp.float32)
    return context.astype(jnp.bfloat16).reshape(new_tokens, head_count * LATENT)


def reference(queries, suffix_latent, page_pool, page_owner, page_slot, prefix_len, moe_input, expert_ids, gate_weights, w_gate, w_up, w_down):
    page_rows = page_pool.reshape(REQS * PAGES_DEV, PAGE, KD)
    query_blocks = queries.reshape(REQS, TQ, HEADS * KD)
    suffix_blocks = suffix_latent.reshape(REQS, TQ, KD)

    def one_request(inputs):
        query_rows, suffix_rows, owners, slot_ids, length = inputs
        rows_wanted = (owners * PAGES_DEV + slot_ids).astype(jnp.int32)
        prefix_keys = page_rows[rows_wanted].reshape(PMAX * PAGE, KD)
        return attend(query_rows, suffix_rows, prefix_keys, length)

    contexts = lax.map(one_request, (query_blocks, suffix_blocks, page_owner, page_slot, prefix_len))
    attn_context = contexts.reshape(TOK_A, HEADS * LATENT)

    block_count = TOK_M // TM
    routed = expert_ids.reshape(block_count, TM * TOP)
    onehot = (routed[:, :, None] == jnp.arange(EXPERTS, dtype=jnp.int32)[None, None, :]).astype(jnp.int32)
    slot_index = jnp.sum((jnp.cumsum(onehot, axis=1) - 1) * onehot, axis=2)
    position = (jnp.arange(block_count, dtype=jnp.int32)[:, None] * CAP + slot_index).reshape(-1).astype(jnp.int32)
    token_index = (jnp.arange(block_count * TM * TOP, dtype=jnp.int32) // TOP).astype(jnp.int32)
    flat_routed = routed.reshape(-1)
    row_table = jnp.full((EXPERTS, block_count * CAP), TOK_M, jnp.int32).at[flat_routed, position].set(token_index)
    weight_table = jnp.zeros((EXPERTS, block_count * CAP), jnp.float32).at[flat_routed, position].set(gate_weights.reshape(-1))
    padded = jnp.concatenate([moe_input, jnp.zeros((1, HID), moe_input.dtype)], axis=0)

    def one_expert(accumulated, inputs):
        rows_used, row_weight, gate_matrix, up_matrix, down_matrix = inputs
        chosen_rows = padded[rows_used]
        gate_proj = jnp.dot(chosen_rows, gate_matrix, preferred_element_type=jnp.float32)
        up_proj = jnp.dot(chosen_rows, up_matrix, preferred_element_type=jnp.float32)
        hidden = (jax.nn.silu(gate_proj) * up_proj).astype(jnp.bfloat16)
        expert_out = jnp.dot(hidden, down_matrix, preferred_element_type=jnp.float32).astype(jnp.bfloat16)
        accumulated = accumulated.at[rows_used].add(row_weight[:, None] * expert_out.astype(jnp.float32))
        return accumulated, None

    accumulated, unused = lax.scan(one_expert, jnp.zeros((TOK_M + 1, HID), jnp.float32), (row_table, weight_table, w_gate, w_up, w_down))
    moe_output = accumulated[:TOK_M].astype(jnp.bfloat16)
    return attn_context, moe_output
```

```python
import functools
import math

import jax
import jax.numpy as jnp
from jax import lax
from jax.experimental import pallas as pl
from jax.experimental.pallas import tpu as pltpu
from jax.sharding import PartitionSpec as P

LATENT = 512
ROPE = 64
KEY = LATENT + ROPE
PAGE = 64

score_scale = 0.07216878364870322
neg_large = -1e30


def pull(values, axis, stride, size, shift):
    total = lax.axis_size(axis)
    pairs = []
    for dst in range(total):
        pos = (dst // stride) % size
        src = dst + (((pos + shift) % size) - pos) * stride
        pairs.append((src, dst))
    return lax.ppermute(values, axis, pairs)


def push(values, axis, stride, size, shift):
    return pull(values, axis, stride, size, size - shift)


def gather_stages():
    ep_size = lax.axis_size("ep")
    inner = 2 if ep_size % 2 == 0 else 1
    middle = 2 if ep_size % (2 * inner) == 0 else 1
    outer = ep_size // (inner * middle)
    stages = [
        ("ep", inner * middle, outer),
        ("dp", 1, lax.axis_size("dp")),
        ("ep", inner, middle),
        ("ep", 1, inner),
    ]
    return [stage for stage in stages if stage[2] > 1]


def attention_body(bias_ref, q_ref, k_ref, o_ref, *, heads, prefix):
    tokens = q_ref.shape[0]
    suffix = k_ref.shape[0] - prefix
    factor = score_scale * math.log2(math.e)
    bias = bias_ref[...]
    row = lax.broadcasted_iota(jnp.int32, (tokens, suffix), 0)
    col = lax.broadcasted_iota(jnp.int32, (tokens, suffix), 1)
    for h in range(heads):
        q = q_ref[:, h * KEY : (h + 1) * KEY]
        s = lax.dot_general(
            q, k_ref[...], (((1,), (1,)), ((), ())), preferred_element_type=jnp.float32
        )
        sp = s[:, :prefix] + bias
        ss = jnp.where(col <= row, s[:, prefix:], neg_large)
        m = jnp.maximum(jnp.max(sp, axis=1, keepdims=True), jnp.max(ss, axis=1, keepdims=True))
        shift = m * factor
        pp = jnp.exp2(sp * factor - shift)
        ps = jnp.exp2(ss * factor - shift)
        total = jnp.sum(pp, axis=1, keepdims=True) + jnp.sum(ps, axis=1, keepdims=True)
        acc = jnp.dot(
            pp.astype(jnp.bfloat16), k_ref[:prefix, :LATENT], preferred_element_type=jnp.float32
        )
        acc += jnp.dot(
            ps.astype(jnp.bfloat16), k_ref[prefix:, :LATENT], preferred_element_type=jnp.float32
        )
        o_ref[:, h * LATENT : (h + 1) * LATENT] = (acc / total).astype(jnp.bfloat16)


def attend(queries, keys, bias):
    tokens = queries.shape[0]
    head_count = queries.shape[1] // KEY
    prefix = bias.shape[1]
    heads = 2
    return pl.pallas_call(
        functools.partial(attention_body, heads=heads, prefix=prefix),
        grid=(head_count // heads,),
        in_specs=[
            pl.BlockSpec((1, prefix), lambda i: (0, 0)),
            pl.BlockSpec((tokens, heads * KEY), lambda i: (0, i)),
            pl.BlockSpec(keys.shape, lambda i: (0, 0)),
        ],
        out_specs=pl.BlockSpec((tokens, heads * LATENT), lambda i: (0, i)),
        out_shape=jax.ShapeDtypeStruct((tokens, head_count * LATENT), jnp.bfloat16),
        compiler_params=pltpu.CompilerParams(vmem_limit_bytes=56 << 20),
        name="attend",
    )(bias, queries, keys)


def fetch_pages(page_pool, page_owner, page_slot, length):
    ep_size = lax.axis_size("ep")
    dp_size = lax.axis_size("dp")
    me = lax.axis_index("ep")
    plane = lax.axis_index("dp")
    pages = page_owner.shape[1]
    ranks = (pages + ep_size - 1) // ep_size
    planes = dp_size if ranks % dp_size == 0 else 1
    own_ranks = ranks // planes
    page_id = jnp.arange(pages, dtype=jnp.int32)
    owners = jnp.arange(ep_size, dtype=jnp.int32)
    rank_id = jnp.arange(ranks, dtype=jnp.int32)
    match = (page_owner[0][None, None, :] == owners[:, None, None]) & (
        page_id[None, None, :] // ep_size == rank_id[None, :, None]
    )
    wanted = jnp.sum(jnp.where(match, page_slot[0][None, None, :], 0), axis=2)
    asked = lax.all_to_all(wanted, "ep", split_axis=0, concat_axis=0, tiled=True)
    steps = jnp.arange(ep_size, dtype=jnp.int32)
    serve = (me - steps) % ep_size
    slots = asked[serve]
    first = (plane * own_ranks) % ranks if planes > 1 else 0
    mine = lax.dynamic_slice_in_dim(slots, first, own_ranks, axis=1)
    pool = page_pool.reshape(page_pool.shape[0], PAGE, KEY)
    chosen = pool[mine.reshape(-1)].reshape(ep_size, own_ranks * PAGE, KEY)
    pieces = []
    for step in range(ep_size):
        block = chosen[step]
        pieces.append(pull(block, "ep", 1, ep_size, step) if step else block)
    groups = 4
    per = ep_size // groups
    merged = [jnp.concatenate(pieces[g * per : (g + 1) * per], axis=0) for g in range(groups)]
    blocks = list(merged)
    for shift in range(1, planes):
        blocks += [pull(m, "dp", 1, dp_size, shift) for m in merged]
    hear = (me + steps) % ep_size
    number = jnp.sum(jnp.where(match, page_id[None, None, :], 0), axis=2)
    number = jnp.where(jnp.any(match, axis=2), number, pages)[hear]
    by_plane = number.reshape(ep_size, planes, own_ranks).transpose(1, 0, 2)
    if planes > 1:
        by_plane = by_plane[(plane + jnp.arange(planes, dtype=jnp.int32)) % planes]
    position = by_plane.reshape(-1)[:, None] * PAGE + jnp.arange(PAGE, dtype=jnp.int32)[None, :]
    seen = (position < length) & (position < pages * PAGE)
    bias = jnp.where(seen, 0.0, neg_large).astype(jnp.float32).reshape(1, -1)
    return blocks, bias


def split_exact(values):
    high = values.astype(jnp.bfloat16)
    rest = values - high.astype(jnp.float32)
    mid = rest.astype(jnp.bfloat16)
    low = (rest - mid.astype(jnp.float32)).astype(jnp.bfloat16)
    return jnp.concatenate([high, mid, low], axis=1)


def experts_part(moe_input, expert_ids, gate_weights, w_gate, w_up, w_down):
    ep_size = lax.axis_size("ep")
    tokens, features = moe_input.shape
    experts = jnp.arange(ep_size, dtype=jnp.int32)
    named = expert_ids[:, :, None] == experts[None, None, :]
    dense = jnp.sum(jnp.where(named, gate_weights[:, :, None], 0.0), axis=1)
    extra = split_exact(dense)
    lanes = -(-extra.shape[1] // 128) * 128
    extra = jnp.pad(extra, ((0, 0), (0, lanes - extra.shape[1])))
    rows = jnp.concatenate([moe_input, extra], axis=1)
    stages = gather_stages()
    for axis, stride, size in stages:
        rows = jnp.concatenate(
            [rows] + [pull(rows, axis, stride, size, shift) for shift in range(1, size)], axis=0
        )
    inputs = rows[:, :features]
    parts = rows[:, features : features + 3 * ep_size].astype(jnp.float32)
    parts = parts.reshape(-1, 3, ep_size)
    here = (experts == lax.axis_index("ep"))[None, None, :]
    parts = jnp.sum(jnp.where(here, parts, 0.0), axis=2)
    weight = (parts[:, 0] + parts[:, 1] + parts[:, 2])[:, None]
    gate_proj = jnp.dot(inputs, w_gate[0], preferred_element_type=jnp.float32)
    up_proj = jnp.dot(inputs, w_up[0], preferred_element_type=jnp.float32)
    hidden = (jax.nn.silu(gate_proj) * up_proj).astype(jnp.bfloat16)
    kept = jnp.dot(hidden, w_down[0], preferred_element_type=jnp.float32) * weight
    for axis, stride, size in reversed(stages):
        count = kept.shape[0] // size
        moved = [
            push(kept[s * count : (s + 1) * count].astype(jnp.bfloat16), axis, stride, size, s)
            for s in range(1, size)
        ]
        kept = kept[:count]
        for m in moved:
            kept = kept + m.astype(jnp.float32)
    return kept.astype(jnp.bfloat16)


def on_device(
    queries,
    suffix_latent,
    page_pool,
    page_owner,
    page_slot,
    prefix_len,
    moe_input,
    expert_ids,
    gate_weights,
    w_gate,
    w_up,
    w_down,
):
    blocks, bias = fetch_pages(page_pool, page_owner, page_slot, prefix_len[0])
    moe_output = experts_part(moe_input, expert_ids, gate_weights, w_gate, w_up, w_down)
    keys = jnp.concatenate(blocks + [suffix_latent], axis=0)
    attn_context = attend(queries, keys, bias)
    return (attn_context, moe_output)


def solution(mesh):
    return jax.shard_map(
        on_device,
        mesh=mesh,
        in_specs=(
            P("ep", "dp"),
            P("ep", None),
            P("ep", None),
            P("ep", None),
            P("ep", None),
            P("ep"),
            P(("dp", "ep"), None),
            P(("dp", "ep"), None),
            P(("dp", "ep"), None),
            P("ep", None, "dp"),
            P("ep", None, "dp"),
            P("ep", "dp", None),
        ),
        out_specs=(P("ep", "dp"), P(("dp", "ep"), None)),
        check_vma=False,
    )
```

```python
import functools
import math

import jax
import jax.numpy as jnp
from jax import lax
from jax.experimental import pallas as pl
from jax.experimental.pallas import tpu as pltpu
from jax.sharding import PartitionSpec as P


LATENT = 512
ROPE = 64
KEY = LATENT + ROPE
PAGE = 64

score_scale = 0.07216878364870322
neg_large = -1e30


def pull(values, axis, stride, size, shift):
    total = lax.axis_size(axis)
    pairs = []
    for dst in range(total):
        pos = (dst // stride) % size
        src = dst + (((pos + shift) % size) - pos) * stride
        pairs.append((src, dst))
    return lax.ppermute(values, axis, pairs)


def push(values, axis, stride, size, shift):
    return pull(values, axis, stride, size, size - shift)


def gather_stages():
    ep_size = lax.axis_size("ep")
    inner = 2 if ep_size % 2 == 0 else 1
    middle = 2 if ep_size % (2 * inner) == 0 else 1
    outer = ep_size // (inner * middle)
    stages = [
        ("ep", inner * middle, outer),
        ("dp", 1, lax.axis_size("dp")),
        ("ep", inner, middle),
        ("ep", 1, inner),
    ]
    return [stage for stage in stages if stage[2] > 1]


def attention_body(bias_ref, q_ref, *refs, heads, together, pieces, aliased):
    piece_refs = refs[:pieces]
    o_ref, k_ref, sem = refs[pieces + aliased :]
    tokens = q_ref.shape[0]
    keys = k_ref.shape[0]
    prefix = bias_ref.shape[1]
    factor = score_scale * math.log2(math.e)

    @pl.when(pl.program_id(0) == 0)
    def load_keys():
        copies = []
        start = 0
        for n, piece in enumerate(piece_refs):
            rows = piece.shape[0]
            copy = pltpu.make_async_copy(piece, k_ref.at[pl.ds(start, rows)], sem.at[n])
            copy.start()
            copies.append(copy)
            start += rows
        for copy in copies:
            copy.wait()

    bias = bias_ref[...]
    row = lax.broadcasted_iota(jnp.int32, (tokens, keys - prefix), 0)
    col = lax.broadcasted_iota(jnp.int32, (tokens, keys - prefix), 1)
    causal = jnp.where(col <= row, 0.0, neg_large).astype(jnp.float32)
    causal = jnp.concatenate([causal] * together, axis=0)
    for first in range(0, heads, together):
        group = range(first, first + together)
        q = jnp.concatenate([q_ref[:, h * KEY : (h + 1) * KEY] for h in group], axis=0)
        s = lax.dot_general(
            q, k_ref[...], (((1,), (1,)), ((), ())), preferred_element_type=jnp.float32
        )
        sp = s[:, :prefix] + bias
        ss = s[:, prefix:] + causal
        m = jnp.maximum(jnp.max(sp, axis=1, keepdims=True), jnp.max(ss, axis=1, keepdims=True))
        shift = m * factor
        pp = jnp.exp2(sp * factor - shift)
        ps = jnp.exp2(ss * factor - shift)
        total = jnp.sum(pp, axis=1, keepdims=True) + jnp.sum(ps, axis=1, keepdims=True)
        p = jnp.concatenate([pp.astype(jnp.bfloat16), ps.astype(jnp.bfloat16)], axis=1)
        acc = jnp.dot(p, k_ref[:, :LATENT], preferred_element_type=jnp.float32) / total
        for n, h in enumerate(group):
            part = acc[n * tokens : (n + 1) * tokens]
            o_ref[:, h * LATENT : (h + 1) * LATENT] = part.astype(jnp.bfloat16)


def attend(queries, pieces, bias, start, count, heads, so_far=None):
    tokens = queries.shape[0]
    head_count = queries.shape[1] // KEY
    keys = sum(piece.shape[0] for piece in pieces)
    together = 4 if heads % 4 == 0 and keys <= 2304 else 2
    offset = start // heads
    aliased = 0 if so_far is None else 1
    anywhere = pl.BlockSpec(memory_space=pl.ANY)
    extra = [so_far] if aliased else []
    return pl.pallas_call(
        functools.partial(
            attention_body, heads=heads, together=together, pieces=len(pieces), aliased=aliased
        ),
        grid=(count // heads,),
        in_specs=[
            pl.BlockSpec(bias.shape, lambda i: (0, 0)),
            pl.BlockSpec((tokens, heads * KEY), lambda i: (0, i + offset)),
            *[anywhere] * (len(pieces) + aliased),
        ],
        out_specs=pl.BlockSpec((tokens, heads * LATENT), lambda i: (0, i + offset)),
        out_shape=jax.ShapeDtypeStruct((tokens, head_count * LATENT), jnp.bfloat16),
        scratch_shapes=[
            pltpu.VMEM((keys, KEY), jnp.bfloat16),
            pltpu.SemaphoreType.DMA((len(pieces),)),
        ],
        input_output_aliases={2 + len(pieces): 0} if aliased else {},
        compiler_params=pltpu.CompilerParams(vmem_limit_bytes=56 << 20),
        name="attend",
    )(bias, queries, *pieces, *extra)


def pull_block(values, a, b, inner):
    total = lax.axis_size("ep")
    outer = total // inner
    pairs = []
    for dst in range(total):
        src = (dst // inner + a) % outer * inner + (dst % inner + b) % inner
        pairs.append((src, dst))
    return lax.ppermute(values, "ep", pairs)


def fetch_pages(page_pool, page_owner, page_slot, length):
    ep_size = lax.axis_size("ep")
    dp_size = lax.axis_size("dp")
    me = lax.axis_index("ep")
    plane = lax.axis_index("dp")
    pages = page_owner.shape[1]
    ranks = (pages + ep_size - 1) // ep_size
    planes = dp_size if ranks % dp_size == 0 else 1
    own_ranks = ranks // planes
    inner = 4 if ep_size % 4 == 0 else 1
    outer = ep_size // inner
    page_id = jnp.arange(pages, dtype=jnp.int32)
    owners = jnp.arange(ep_size, dtype=jnp.int32)
    rank_id = jnp.arange(ranks, dtype=jnp.int32)
    match = (page_owner[0][None, None, :] == owners[:, None, None]) & (
        page_id[None, None, :] // ep_size == rank_id[None, :, None]
    )
    wanted = jnp.sum(jnp.where(match, page_slot[0][None, None, :], 0), axis=2)
    asked = lax.all_to_all(wanted, "ep", split_axis=0, concat_axis=0, tiled=True)
    steps = jnp.arange(ep_size, dtype=jnp.int32)
    serve = (me // inner - steps // inner) % outer * inner + (me % inner - steps % inner) % inner
    hear = (me // inner + steps // inner) % outer * inner + (me % inner + steps % inner) % inner
    slots = asked[serve]
    first = (plane * own_ranks) % ranks if planes > 1 else 0
    mine = lax.dynamic_slice_in_dim(slots, first, own_ranks, axis=1)
    pool = page_pool.reshape(page_pool.shape[0], PAGE, KEY)
    chosen = pick_pages(pool, mine, ep_size, own_ranks)
    pieces = []
    for step in range(ep_size):
        a, b = step // inner, step % inner
        pieces.append(pull_block(chosen[step], a, b, inner) if step else chosen[step])
    blocks = list(pieces)
    for shift in range(1, planes):
        for step in range(ep_size):
            blocks.append(pull(pieces[step], "dp", 1, dp_size, shift))
    number = jnp.sum(jnp.where(match, page_id[None, None, :], 0), axis=2)
    number = jnp.where(jnp.any(match, axis=2), number, pages)[hear]
    by_plane = number.reshape(ep_size, planes, own_ranks).transpose(1, 0, 2)
    if planes > 1:
        by_plane = by_plane[(plane + jnp.arange(planes, dtype=jnp.int32)) % planes]
    position = by_plane.reshape(-1)[:, None] * PAGE + jnp.arange(PAGE, dtype=jnp.int32)[None, :]
    seen = (position < length) & (position < pages * PAGE)
    bias = jnp.where(seen, 0.0, neg_large).astype(jnp.float32).reshape(1, -1)
    return blocks, bias


def pick_body(slots_ref, pool_ref, *refs, count):
    outs = refs[:-1]
    sem = refs[-1]
    copies = []
    for n, out in enumerate(outs):
        for r in range(count):
            copies.append(
                pltpu.make_async_copy(
                    pool_ref.at[slots_ref[n, r]], out.at[pl.ds(r * PAGE, PAGE)], sem.at[n, r]
                )
            )
    for copy in copies:
        copy.start()
    for copy in copies:
        copy.wait()


def pick_pages(pool, slots, steps, count):
    anywhere = pl.BlockSpec(memory_space=pl.ANY)
    return pl.pallas_call(
        functools.partial(pick_body, count=count),
        in_specs=[pl.BlockSpec(memory_space=pltpu.SMEM), anywhere],
        out_specs=[anywhere] * steps,
        out_shape=[jax.ShapeDtypeStruct((count * PAGE, KEY), pool.dtype)] * steps,
        scratch_shapes=[pltpu.SemaphoreType.DMA((steps, count))],
        name="pick",
    )(slots, pool)


def split_exact(values):
    high = values.astype(jnp.bfloat16)
    rest = values - high.astype(jnp.float32)
    mid = rest.astype(jnp.bfloat16)
    low = (rest - mid.astype(jnp.float32)).astype(jnp.bfloat16)
    return jnp.concatenate([high, mid, low], axis=1)


def experts_staged(moe_input, expert_ids, gate_weights, w_gate, w_up, w_down):
    ep_size = lax.axis_size("ep")
    _, features = moe_input.shape
    experts = jnp.arange(ep_size, dtype=jnp.int32)
    named = expert_ids[:, :, None] == experts[None, None, :]
    dense = jnp.sum(jnp.where(named, gate_weights[:, :, None], 0.0), axis=1)
    extra = split_exact(dense)
    lanes = -(-extra.shape[1] // 128) * 128
    extra = jnp.pad(extra, ((0, 0), (0, lanes - extra.shape[1])))
    rows = jnp.concatenate([moe_input, extra], axis=1)
    stages = gather_stages()
    for axis, stride, size in stages:
        rows = jnp.concatenate(
            [rows] + [pull(rows, axis, stride, size, shift) for shift in range(1, size)], axis=0
        )
    inputs = rows[:, :features]
    parts = rows[:, features : features + 3 * ep_size].astype(jnp.float32)
    parts = parts.reshape(-1, 3, ep_size)
    here = (experts == lax.axis_index("ep"))[None, None, :]
    parts = jnp.sum(jnp.where(here, parts, 0.0), axis=2)
    weight = (parts[:, 0] + parts[:, 1] + parts[:, 2])[:, None]
    gate_proj = jnp.dot(inputs, w_gate[0], preferred_element_type=jnp.float32)
    up_proj = jnp.dot(inputs, w_up[0], preferred_element_type=jnp.float32)
    hidden = (jax.nn.silu(gate_proj) * up_proj).astype(jnp.bfloat16)
    kept = jnp.dot(hidden, w_down[0], preferred_element_type=jnp.float32) * weight
    for axis, stride, size in reversed(stages):
        count = kept.shape[0] // size
        moved = [
            push(kept[s * count : (s + 1) * count].astype(jnp.bfloat16), axis, stride, size, s)
            for s in range(1, size)
        ]
        kept = kept[:count]
        for m in moved:
            kept = kept + m.astype(jnp.float32)
    return kept.astype(jnp.bfloat16)


def expert_body(weight_ref, *refs, places, hidden_steps):
    pieces = refs[: len(places)]
    gate_ref, up_ref, down_ref, keep_ref, send_ref, x_ref, acc_ref, sem = refs[len(places) :]
    step = pl.program_id(0)

    @pl.when(step == 0)
    def load_rows():
        copies = []
        for n, (piece, (row, lane, lanes)) in enumerate(zip(pieces, places, strict=True)):
            rows = piece.shape[0]
            copies.append(
                pltpu.make_async_copy(
                    piece.at[:, pl.ds(0, lanes)],
                    x_ref.at[pl.ds(row, rows), pl.ds(lane, lanes)],
                    sem.at[n],
                )
            )
        for copy in copies:
            copy.start()
        for copy in copies:
            copy.wait()

    x = x_ref[...]
    gate = jnp.dot(x, gate_ref[...], preferred_element_type=jnp.float32)
    up = jnp.dot(x, up_ref[...], preferred_element_type=jnp.float32)
    hidden = (gate / (1.0 + jnp.exp(-gate)) * up).astype(jnp.bfloat16)
    part = jnp.dot(hidden, down_ref[...], preferred_element_type=jnp.float32)

    @pl.when(step == 0)
    def begin():
        acc_ref[...] = part

    @pl.when((step > 0) & (step < hidden_steps - 1))
    def add():
        acc_ref[...] += part

    @pl.when(step == hidden_steps - 1)
    def finish():
        total = (acc_ref[...] + part) * weight_ref[...]
        half = keep_ref.shape[0]
        keep_ref[...] = total[:half]
        send_ref[...] = total[half:].astype(jnp.bfloat16)


def expert_call(weight, pieces, places, w_gate, w_up, w_down):
    rows = weight.shape[0]
    features, hidden = w_gate.shape
    block = 256
    anywhere = pl.BlockSpec(memory_space=pl.ANY)
    return pl.pallas_call(
        functools.partial(expert_body, places=places, hidden_steps=hidden // block),
        grid=(hidden // block,),
        in_specs=[
            pl.BlockSpec((rows, 1), lambda i: (0, 0)),
            *[anywhere] * len(pieces),
            pl.BlockSpec((features, block), lambda i: (0, i)),
            pl.BlockSpec((features, block), lambda i: (0, i)),
            pl.BlockSpec((block, features), lambda i: (i, 0)),
        ],
        out_specs=[
            pl.BlockSpec((rows // 2, features), lambda i: (0, 0)),
            pl.BlockSpec((rows // 2, features), lambda i: (0, 0)),
        ],
        out_shape=[
            jax.ShapeDtypeStruct((rows // 2, features), jnp.float32),
            jax.ShapeDtypeStruct((rows // 2, features), jnp.bfloat16),
        ],
        scratch_shapes=[
            pltpu.VMEM((rows, features), jnp.bfloat16),
            pltpu.VMEM((rows, features), jnp.float32),
            pltpu.SemaphoreType.DMA((len(pieces),)),
        ],
        compiler_params=pltpu.CompilerParams(vmem_limit_bytes=58 << 20),
        name="expert",
    )(weight, *pieces, w_gate, w_up, w_down)


def can_square(tokens, hidden):
    ep_size = lax.axis_size("ep")
    total = tokens * ep_size * lax.axis_size("dp")
    return lax.axis_size("dp") == 2 and ep_size % 4 == 0 and total <= 512 and hidden % 256 == 0


def experts_square(moe_input, expert_ids, gate_weights, w_gate, w_up, w_down):
    ep_size = lax.axis_size("ep")
    outer = ep_size // 4
    tokens, features = moe_input.shape
    left = features // 256 * 128
    experts = jnp.arange(ep_size, dtype=jnp.int32)
    named = expert_ids[:, :, None] == experts[None, None, :]
    dense = jnp.sum(jnp.where(named, gate_weights[:, :, None], 0.0), axis=1)
    extra = split_exact(dense)
    lanes = -(-extra.shape[1] // 128) * 128
    extra = jnp.pad(extra, ((0, 0), (0, lanes - extra.shape[1])))
    rows = jnp.concatenate([moe_input, extra], axis=1)
    far = []
    for shift in range(1, outer):
        far.append(pull(rows, "ep", 4, outer, shift))
    own = jnp.concatenate([rows] + far, axis=0)
    by_x = pull(own, "dp", 1, 2, 1)
    by_y = pull(own, "ep", 2, 2, 1)
    both_a = pull(by_x[:, :left], "ep", 2, 2, 1)
    both_b = pull(by_y[:, left:], "dp", 1, 2, 1)
    near = [own, by_x, by_y, both_a, both_b]
    partner = []
    for piece in near:
        partner.append(pull(piece, "ep", 1, 2, 1))
    block = own.shape[0]
    places = []
    for base in (0, 4 * block):
        places += [(base + n * block, 0, features) for n in range(3)]
        places += [(base + 3 * block, 0, left), (base + 3 * block, left, features - left)]
    tags = []
    for group in (near, partner):
        tags += [piece[:, features:] for piece in group[:3]] + [group[4][:, features - left :]]
    parts = jnp.concatenate(tags, axis=0)[:, : 3 * ep_size].astype(jnp.float32)
    parts = parts.reshape(-1, 3, ep_size)
    here = (experts == lax.axis_index("ep"))[None, None, :]
    parts = jnp.sum(jnp.where(here, parts, 0.0), axis=2)
    weight = (parts[:, 0] + parts[:, 1] + parts[:, 2])[:, None]
    keep, send = expert_call(
        weight, near + partner, tuple(places), w_gate[0], w_up[0], w_down[0]
    )
    got = pull(send, "ep", 1, 2, 1)
    yield None
    keep = keep + got.astype(jnp.float32)
    own, by_x, by_y, both = (keep[n * block : (n + 1) * block] for n in range(4))
    got_a = pull(both[:, :left].astype(jnp.bfloat16), "ep", 2, 2, 1)
    got_b = pull(both[:, left:].astype(jnp.bfloat16), "dp", 1, 2, 1)
    yield None
    by_x = jnp.concatenate([by_x[:, :left] + got_a.astype(jnp.float32), by_x[:, left:]], axis=1)
    by_y = jnp.concatenate([by_y[:, :left], by_y[:, left:] + got_b.astype(jnp.float32)], axis=1)
    got_x = pull(by_x.astype(jnp.bfloat16), "dp", 1, 2, 1)
    got_y = pull(by_y.astype(jnp.bfloat16), "ep", 2, 2, 1)
    yield None
    own = own + got_x.astype(jnp.float32) + got_y.astype(jnp.float32)
    got = []
    for shift in range(1, outer):
        piece = own[shift * tokens : (shift + 1) * tokens].astype(jnp.bfloat16)
        got.append(push(piece, "ep", 4, outer, shift))
    yield None
    total = own[:tokens]
    for piece in got:
        total = total + piece.astype(jnp.float32)
    yield total.astype(jnp.bfloat16)


def on_device(
    queries,
    suffix_latent,
    page_pool,
    page_owner,
    page_slot,
    prefix_len,
    moe_input,
    expert_ids,
    gate_weights,
    w_gate,
    w_up,
    w_down,
):
    pieces, bias = fetch_pages(page_pool, page_owner, page_slot, prefix_len[0])
    pieces = pieces + [suffix_latent]
    moe_args = (moe_input, expert_ids, gate_weights, w_gate, w_up, w_down)
    head_count = queries.shape[1] // KEY
    if not can_square(moe_input.shape[0], w_gate.shape[2]):
        moe_output = experts_staged(*moe_args)
        return (attend(queries, pieces, bias, 0, head_count, 2), moe_output)
    stages = experts_square(*moe_args)
    heads = 4
    steps = head_count // heads
    cuts = [0, steps // 8, 3 * steps // 8, 6 * steps // 8, steps]
    attn_context = None
    for n in range(4):
        next(stages)
        start, count = cuts[n] * heads, (cuts[n + 1] - cuts[n]) * heads
        if count:
            attn_context = attend(
                queries, pieces, bias, start, count, heads, attn_context
            )
    moe_output = next(stages)
    return (attn_context, moe_output)


def solution(mesh):
    return jax.shard_map(
        on_device,
        mesh=mesh,
        in_specs=(
            P("ep", "dp"),
            P("ep", None),
            P("ep", None),
            P("ep", None),
            P("ep", None),
            P("ep"),
            P(("dp", "ep"), None),
            P(("dp", "ep"), None),
            P(("dp", "ep"), None),
            P("ep", None, "dp"),
            P("ep", None, "dp"),
            P("ep", "dp", None),
        ),
        out_specs=(P("ep", "dp"), P(("dp", "ep"), None)),
        check_vma=False,
    )
```

```python
import functools
import math

import jax
import jax.numpy as jnp
from jax import lax
from jax.experimental import pallas as pl
from jax.experimental.pallas import tpu as pltpu
from jax.sharding import PartitionSpec as P


LATENT = 512
ROPE = 64
KEY = LATENT + ROPE
PAGE = 64

score_scale = 0.07216878364870322
neg_large = -1e30


def partner(pos, shift, size):
    return pos ^ shift if size & (size - 1) == 0 else (pos + shift) % size


def pull(values, axis, stride, size, shift, back=False):
    total = lax.axis_size(axis)
    pairs = []
    for dst in range(total):
        pos = (dst // stride) % size
        src = dst + (partner(pos, shift, size) - pos) * stride
        pairs.append((dst, src) if back else (src, dst))
    return lax.ppermute(values, axis, pairs)


def push(values, axis, stride, size, shift):
    return pull(values, axis, stride, size, shift, back=True)


def gather_stages():
    ep_size = lax.axis_size("ep")
    inner = 2 if ep_size % 2 == 0 else 1
    middle = 2 if ep_size % (2 * inner) == 0 else 1
    outer = ep_size // (inner * middle)
    stages = [
        ("ep", inner * middle, outer),
        ("dp", 1, lax.axis_size("dp")),
        ("ep", inner, middle),
        ("ep", 1, inner),
    ]
    return [stage for stage in stages if stage[2] > 1]


def attention_body(
    number_ref, length_ref, q_ref, *refs, heads, together, pieces, aliased
):
    piece_refs = refs[:pieces]
    o_ref, k_ref, bias_ref, sem = refs[pieces + aliased :]
    tokens = q_ref.shape[0]
    keys = k_ref.shape[0]
    prefix = bias_ref.shape[1]
    factor = score_scale * math.log2(math.e)

    @pl.when(pl.program_id(0) == 0)
    def load_keys():
        copies = []
        start = 0
        for n, piece in enumerate(piece_refs):
            rows = piece.shape[0]
            copy = pltpu.make_async_copy(piece, k_ref.at[pl.ds(start, rows)], sem.at[n])
            copy.start()
            copies.append(copy)
            start += rows
        lane = lax.broadcasted_iota(jnp.int32, (1, 2 * PAGE), 1)
        for pair in range(prefix // (2 * PAGE)):
            low = number_ref[2 * pair] * PAGE
            high = number_ref[2 * pair + 1] * PAGE - PAGE
            position = lane + jnp.where(lane < PAGE, low, high)
            seen = jnp.where(position < length_ref[0], 0.0, neg_large)
            bias_ref[:, 2 * PAGE * pair : 2 * PAGE * (pair + 1)] = seen.astype(jnp.float32)
        for copy in copies:
            copy.wait()

    bias = bias_ref[...]
    row = lax.broadcasted_iota(jnp.int32, (tokens, keys - prefix), 0)
    col = lax.broadcasted_iota(jnp.int32, (tokens, keys - prefix), 1)
    causal = jnp.where(col <= row, 0.0, neg_large).astype(jnp.float32)
    causal = jnp.concatenate([causal] * together, axis=0)
    for first in range(0, heads, together):
        group = range(first, first + together)
        q = jnp.concatenate([q_ref[:, h * KEY : (h + 1) * KEY] for h in group], axis=0)
        s = lax.dot_general(
            q, k_ref[...], (((1,), (1,)), ((), ())), preferred_element_type=jnp.float32
        )
        sp = s[:, :prefix] + bias
        ss = s[:, prefix:] + causal
        m = jnp.maximum(jnp.max(sp, axis=1, keepdims=True), jnp.max(ss, axis=1, keepdims=True))
        shift = m * factor
        pp = jnp.exp2(sp * factor - shift)
        ps = jnp.exp2(ss * factor - shift)
        total = jnp.sum(pp, axis=1, keepdims=True) + jnp.sum(ps, axis=1, keepdims=True)
        p = jnp.concatenate([pp.astype(jnp.bfloat16), ps.astype(jnp.bfloat16)], axis=1)
        acc = jnp.dot(p, k_ref[:, :LATENT], preferred_element_type=jnp.float32) / total
        for n, h in enumerate(group):
            part = acc[n * tokens : (n + 1) * tokens]
            o_ref[:, h * LATENT : (h + 1) * LATENT] = part.astype(jnp.bfloat16)


def attend(queries, pieces, numbers, length, start, count, heads, so_far=None):
    tokens = queries.shape[0]
    head_count = queries.shape[1] // KEY
    keys = sum(piece.shape[0] for piece in pieces)
    prefix = numbers.shape[0] * PAGE
    scalars = pl.BlockSpec(memory_space=pltpu.SMEM)
    together = 4 if heads % 4 == 0 and keys <= 2304 else 2
    offset = start // heads
    aliased = 0 if so_far is None else 1
    anywhere = pl.BlockSpec(memory_space=pl.ANY)
    extra = [so_far] if aliased else []
    return pl.pallas_call(
        functools.partial(
            attention_body, heads=heads, together=together, pieces=len(pieces), aliased=aliased
        ),
        grid=(count // heads,),
        in_specs=[
            scalars,
            scalars,
            pl.BlockSpec((tokens, heads * KEY), lambda i: (0, i + offset)),
            *[anywhere] * (len(pieces) + aliased),
        ],
        out_specs=pl.BlockSpec((tokens, heads * LATENT), lambda i: (0, i + offset)),
        out_shape=jax.ShapeDtypeStruct((tokens, head_count * LATENT), jnp.bfloat16),
        scratch_shapes=[
            pltpu.VMEM((keys, KEY), jnp.bfloat16),
            pltpu.VMEM((1, prefix), jnp.float32),
            pltpu.SemaphoreType.DMA((len(pieces),)),
        ],
        input_output_aliases={3 + len(pieces): 0} if aliased else {},
        compiler_params=pltpu.CompilerParams(vmem_limit_bytes=56 << 20),
        name="attend",
    )(numbers, length, queries, *pieces, *extra)


def pull_block(values, a, b, inner):
    total = lax.axis_size("ep")
    outer = total // inner
    pairs = []
    for dst in range(total):
        src = partner(dst // inner, a, outer) * inner + partner(dst % inner, b, inner)
        pairs.append((src, dst))
    return lax.ppermute(values, "ep", pairs)


def fetch_pages(page_pool, page_owner, page_slot):
    ep_size = lax.axis_size("ep")
    dp_size = lax.axis_size("dp")
    me = lax.axis_index("ep")
    plane = lax.axis_index("dp")
    pages = page_owner.shape[1]
    ranks = (pages + ep_size - 1) // ep_size
    planes = dp_size if ranks % dp_size == 0 else 1
    own_ranks = ranks // planes
    inner = 4 if ep_size % 4 == 0 else 1
    outer = ep_size // inner
    page_id = jnp.arange(pages, dtype=jnp.int32)
    owners = jnp.arange(ep_size, dtype=jnp.int32)
    rank_id = jnp.arange(ranks, dtype=jnp.int32)
    match = (page_owner[0][None, None, :] == owners[:, None, None]) & (
        page_id[None, None, :] // ep_size == rank_id[None, :, None]
    )
    wanted = jnp.sum(jnp.where(match, page_slot[0][None, None, :], 0), axis=2)
    asked = lax.all_to_all(wanted, "ep", split_axis=0, concat_axis=0, tiled=True)
    first = (plane * own_ranks) % ranks if planes > 1 else 0
    pool = page_pool.reshape(page_pool.shape[0], PAGE, KEY)
    where = jnp.stack([me, jnp.asarray(first, jnp.int32)]).astype(jnp.int32)
    chosen = pick_pages(where, asked, pool, inner, own_ranks)
    groups = []
    for a in range(outer):
        pieces = []
        for b in range(inner):
            step = a * inner + b
            pieces.append(pull_block(chosen[step], a, b, inner) if step else chosen[0])
        groups.append(pack_pages(pieces))
    blocks = list(groups)
    for shift in range(1, planes):
        for a in range(outer):
            blocks.append(pull(groups[a], "dp", 1, dp_size, shift))
    steps = jnp.arange(ep_size, dtype=jnp.int32)
    group, place = me // inner, me % inner
    hear = partner(group, steps // inner, outer) * inner + partner(place, steps % inner, inner)
    turn = partner(plane, jnp.arange(planes, dtype=jnp.int32), planes) if planes > 1 else 0
    order = turn * own_ranks + jnp.arange(own_ranks, dtype=jnp.int32)[:, None]
    order = order.T.reshape(planes, 1, own_ranks)
    seat = page_owner[0] + page_id // ep_size * ep_size
    place_of = (hear[None, :, None] + order * ep_size).reshape(-1, 1)
    hit = place_of == seat[None, :]
    numbers = pages + jnp.sum(jnp.where(hit, page_id[None, :] - pages, 0), axis=1)
    return blocks, numbers


def pack_body(*refs):
    start = 0
    for piece in refs[:-1]:
        rows = piece.shape[0]
        refs[-1][start : start + rows] = piece[...]
        start += rows


def pack_pages(pieces):
    if len(pieces) == 1:
        return pieces[0]
    rows = sum(piece.shape[0] for piece in pieces)
    whole = pl.BlockSpec(memory_space=pltpu.VMEM)
    return pl.pallas_call(
        pack_body,
        in_specs=[whole] * len(pieces),
        out_specs=whole,
        out_shape=jax.ShapeDtypeStruct((rows, pieces[0].shape[1]), pieces[0].dtype),
        name="pack",
    )(*pieces)


def pick_body(where_ref, asked_ref, pool_ref, *outs, inner, count):
    steps = len(outs)
    me = where_ref[0]
    for n, out in enumerate(outs):
        low, high = n % inner, n // inner
        if inner & (inner - 1) == 0:
            place = (me % inner) ^ low
        else:
            place = (me % inner + inner - low) % inner
        outer = steps // inner
        if outer & (outer - 1) == 0:
            group = (me // inner) ^ high
        else:
            group = (me // inner + outer - high) % outer
        for r in range(count):
            slot = asked_ref[group * inner + place, where_ref[1] + r]
            out[r * PAGE : (r + 1) * PAGE] = pool_ref[slot]


def pick_pages(where, asked, pool, inner, count):
    steps = asked.shape[0]
    scalars = pl.BlockSpec(memory_space=pltpu.SMEM)
    return pl.pallas_call(
        functools.partial(pick_body, inner=inner, count=count),
        in_specs=[scalars, scalars, pl.BlockSpec(memory_space=pltpu.VMEM)],
        out_specs=[pl.BlockSpec(memory_space=pltpu.VMEM)] * steps,
        out_shape=[jax.ShapeDtypeStruct((count * PAGE, KEY), pool.dtype)] * steps,
        name="pick",
    )(where, asked, pool)


def split_exact(values):
    high = values.astype(jnp.bfloat16)
    rest = values - high.astype(jnp.float32)
    mid = rest.astype(jnp.bfloat16)
    low = (rest - mid.astype(jnp.float32)).astype(jnp.bfloat16)
    return jnp.concatenate([high, mid, low], axis=1)


def experts_staged(moe_input, expert_ids, gate_weights, w_gate, w_up, w_down):
    ep_size = lax.axis_size("ep")
    _, features = moe_input.shape
    experts = jnp.arange(ep_size, dtype=jnp.int32)
    named = expert_ids[:, :, None] == experts[None, None, :]
    dense = jnp.sum(jnp.where(named, gate_weights[:, :, None], 0.0), axis=1)
    extra = split_exact(dense)
    lanes = -(-extra.shape[1] // 128) * 128
    extra = jnp.pad(extra, ((0, 0), (0, lanes - extra.shape[1])))
    rows = jnp.concatenate([moe_input, extra], axis=1)
    stages = gather_stages()
    for axis, stride, size in stages:
        rows = jnp.concatenate(
            [rows] + [pull(rows, axis, stride, size, shift) for shift in range(1, size)], axis=0
        )
    inputs = rows[:, :features]
    parts = rows[:, features : features + 3 * ep_size].astype(jnp.float32)
    parts = parts.reshape(-1, 3, ep_size)
    here = (experts == lax.axis_index("ep"))[None, None, :]
    parts = jnp.sum(jnp.where(here, parts, 0.0), axis=2)
    weight = (parts[:, 0] + parts[:, 1] + parts[:, 2])[:, None]
    gate_proj = jnp.dot(inputs, w_gate[0], preferred_element_type=jnp.float32)
    up_proj = jnp.dot(inputs, w_up[0], preferred_element_type=jnp.float32)
    hidden = (jax.nn.silu(gate_proj) * up_proj).astype(jnp.bfloat16)
    kept = jnp.dot(hidden, w_down[0], preferred_element_type=jnp.float32) * weight
    for axis, stride, size in reversed(stages):
        count = kept.shape[0] // size
        moved = [
            push(kept[s * count : (s + 1) * count].astype(jnp.bfloat16), axis, stride, size, s)
            for s in range(1, size)
        ]
        kept = kept[:count]
        for m in moved:
            kept = kept + m.astype(jnp.float32)
    return kept.astype(jnp.bfloat16)


def expert_body(me_ref, *refs, places, hidden_steps, experts, features):
    pieces = refs[: len(places)]
    gate_ref, up_ref, down_ref, keep_ref, send_ref, x_ref, h_ref, w_ref, sem = refs[len(places) :]
    step = pl.program_id(0)

    @pl.when(step == 0)
    def load_rows():
        copies = []
        for n, (piece, (row, lane)) in enumerate(zip(pieces, places, strict=True)):
            rows, lanes = piece.shape
            copies.append(
                pltpu.make_async_copy(
                    piece, x_ref.at[pl.ds(row, rows), pl.ds(lane, lanes)], sem.at[n]
                )
            )
        for copy in copies:
            copy.start()
        for copy in copies:
            copy.wait()
        tags = x_ref[:, features:].astype(jnp.float32)
        lane = lax.broadcasted_iota(jnp.int32, tags.shape, 1)
        mine = (lane % experts == me_ref[0]) & (lane < 3 * experts)
        w_ref[...] = jnp.sum(jnp.where(mine, tags, 0.0), axis=1, keepdims=True)

    block = gate_ref.shape[1]
    for n in range(hidden_steps):

        @pl.when(step == n)
        def first_layer(n=n):
            x = x_ref[:, :features]
            gate = jnp.dot(x, gate_ref[...], preferred_element_type=jnp.float32)
            up = jnp.dot(x, up_ref[...], preferred_element_type=jnp.float32)
            hidden = gate / (1.0 + jnp.exp(-gate)) * up
            h_ref[:, n * block : (n + 1) * block] = hidden.astype(jnp.bfloat16)

    @pl.when(step >= hidden_steps)
    def second_layer():
        part = jnp.dot(h_ref[...], down_ref[...], preferred_element_type=jnp.float32)
        total = part * w_ref[...]
        half = keep_ref.shape[0]
        keep_ref[...] = total[:half]
        send_ref[...] = total[half:].astype(jnp.bfloat16)


def expert_call(me, pieces, places, rows, experts, w_gate, w_up, w_down):
    features, hidden = w_gate.shape
    width = pieces[0].shape[1]
    block = 256
    wide = 512 if features % 512 == 0 else 128
    steps = hidden // block
    anywhere = pl.BlockSpec(memory_space=pl.ANY)
    outs = pl.BlockSpec((rows // 2, wide), lambda i: (0, jnp.maximum(i - steps, 0)))
    return pl.pallas_call(
        functools.partial(
            expert_body, places=places, hidden_steps=steps, experts=experts, features=features
        ),
        grid=(steps + features // wide,),
        in_specs=[
            pl.BlockSpec(memory_space=pltpu.SMEM),
            *[anywhere] * len(pieces),
            pl.BlockSpec((features, block), lambda i: (0, jnp.minimum(i, steps - 1))),
            pl.BlockSpec((features, block), lambda i: (0, jnp.minimum(i, steps - 1))),
            pl.BlockSpec((hidden, wide), lambda i: (0, jnp.maximum(i - steps, 0))),
        ],
        out_specs=[outs, outs],
        out_shape=[
            jax.ShapeDtypeStruct((rows // 2, features), jnp.float32),
            jax.ShapeDtypeStruct((rows // 2, features), jnp.bfloat16),
        ],
        scratch_shapes=[
            pltpu.VMEM((rows, width), jnp.bfloat16),
            pltpu.VMEM((rows, hidden), jnp.bfloat16),
            pltpu.VMEM((rows, 1), jnp.float32),
            pltpu.SemaphoreType.DMA((len(pieces),)),
        ],
        compiler_params=pltpu.CompilerParams(vmem_limit_bytes=58 << 20),
        name="expert",
    )(me, *pieces, w_gate, w_up, w_down)


def can_square(tokens, hidden):
    ep_size = lax.axis_size("ep")
    total = tokens * ep_size * lax.axis_size("dp")
    return lax.axis_size("dp") == 2 and ep_size % 4 == 0 and total <= 512 and hidden % 256 == 0


def experts_square(moe_input, expert_ids, gate_weights, w_gate, w_up, w_down):
    ep_size = lax.axis_size("ep")
    outer = ep_size // 4
    tokens, features = moe_input.shape
    left = features // 256 * 128
    experts = jnp.arange(ep_size, dtype=jnp.int32)
    named = expert_ids[:, :, None] == experts[None, None, :]
    dense = jnp.sum(jnp.where(named, gate_weights[:, :, None], 0.0), axis=1)
    extra = split_exact(dense)
    lanes = -(-extra.shape[1] // 128) * 128
    extra = jnp.pad(extra, ((0, 0), (0, lanes - extra.shape[1])))
    rows = jnp.concatenate([moe_input, extra], axis=1)
    far = []
    for shift in range(1, outer):
        far.append(pull(rows, "ep", 4, outer, shift))
    own = jnp.concatenate([rows] + far, axis=0)
    by_x = pull(own, "dp", 1, 2, 1)
    by_y = pull(own, "ep", 2, 2, 1)
    both_a = pull(by_x[:, :left], "ep", 2, 2, 1)
    both_b = pull(by_y[:, left:], "dp", 1, 2, 1)
    near = [own, by_x, by_y, both_a, both_b]
    across = []
    for piece in near:
        across.append(pull(piece, "ep", 1, 2, 1))
    block = own.shape[0]
    places = []
    for base in (0, 4 * block):
        places += [(base + n * block, 0) for n in range(3)]
        places += [(base + 3 * block, 0), (base + 3 * block, left)]
    me = lax.axis_index("ep").astype(jnp.int32).reshape(1)
    keep, send = expert_call(
        me, near + across, tuple(places), 8 * block, ep_size, w_gate[0], w_up[0], w_down[0]
    )
    got = pull(send, "ep", 1, 2, 1)
    yield None
    keep = keep + got.astype(jnp.float32)
    own, by_x, by_y, both = (keep[n * block : (n + 1) * block] for n in range(4))
    got_a = pull(both[:, :left].astype(jnp.bfloat16), "ep", 2, 2, 1)
    got_b = pull(both[:, left:].astype(jnp.bfloat16), "dp", 1, 2, 1)
    yield None
    by_x = jnp.concatenate([by_x[:, :left] + got_a.astype(jnp.float32), by_x[:, left:]], axis=1)
    by_y = jnp.concatenate([by_y[:, :left], by_y[:, left:] + got_b.astype(jnp.float32)], axis=1)
    got_x = pull(by_x.astype(jnp.bfloat16), "dp", 1, 2, 1)
    got_y = pull(by_y.astype(jnp.bfloat16), "ep", 2, 2, 1)
    yield None
    own = own + got_x.astype(jnp.float32) + got_y.astype(jnp.float32)
    got = []
    for shift in range(1, outer):
        piece = own[shift * tokens : (shift + 1) * tokens].astype(jnp.bfloat16)
        got.append(push(piece, "ep", 4, outer, shift))
    yield None
    total = own[:tokens]
    for piece in got:
        total = total + piece.astype(jnp.float32)
    yield total.astype(jnp.bfloat16)


def on_device(
    queries,
    suffix_latent,
    page_pool,
    page_owner,
    page_slot,
    prefix_len,
    moe_input,
    expert_ids,
    gate_weights,
    w_gate,
    w_up,
    w_down,
):
    pieces, numbers = fetch_pages(page_pool, page_owner, page_slot)
    pieces = pieces + [suffix_latent]
    moe_args = (moe_input, expert_ids, gate_weights, w_gate, w_up, w_down)
    head_count = queries.shape[1] // KEY
    if not can_square(moe_input.shape[0], w_gate.shape[2]):
        moe_output = experts_staged(*moe_args)
        return (attend(queries, pieces, numbers, prefix_len, 0, head_count, 2), moe_output)
    stages = experts_square(*moe_args)
    heads = 4
    steps = head_count // heads
    cuts = [0, steps // 8, 3 * steps // 8, 6 * steps // 8, steps]
    attn_context = None
    for n in range(4):
        next(stages)
        start, count = cuts[n] * heads, (cuts[n + 1] - cuts[n]) * heads
        if count:
            attn_context = attend(
                queries, pieces, numbers, prefix_len, start, count, heads, attn_context
            )
    moe_output = next(stages)
    return (attn_context, moe_output)


def solution(mesh):
    return jax.shard_map(
        on_device,
        mesh=mesh,
        in_specs=(
            P("ep", "dp"),
            P("ep", None),
            P("ep", None),
            P("ep", None),
            P("ep", None),
            P("ep"),
            P(("dp", "ep"), None),
            P(("dp", "ep"), None),
            P(("dp", "ep"), None),
            P("ep", None, "dp"),
            P("ep", None, "dp"),
            P("ep", "dp", None),
        ),
        out_specs=(P("ep", "dp"), P(("dp", "ep"), None)),
        check_vma=False,
    )
```

```python
import functools
import math

import jax
import jax.numpy as jnp
from jax import lax
from jax.experimental import pallas as pl
from jax.experimental.pallas import tpu as pltpu
from jax.sharding import PartitionSpec as P


LATENT = 512
ROPE = 64
KEY = LATENT + ROPE
PAGE = 64
LANES = 128

score_scale = 0.07216878364870322
neg_large = -1e30


def partner(pos, shift, size):
    return pos ^ shift if size & (size - 1) == 0 else (pos + shift) % size


def pull(values, axis, stride, size, shift, back=False):
    total = lax.axis_size(axis)
    pairs = []
    for dst in range(total):
        pos = (dst // stride) % size
        src = dst + (partner(pos, shift, size) - pos) * stride
        pairs.append((dst, src) if back else (src, dst))
    return lax.ppermute(values, axis, pairs)


def push(values, axis, stride, size, shift):
    return pull(values, axis, stride, size, shift, back=True)


def gather_stages():
    ep_size = lax.axis_size("ep")
    inner = 2 if ep_size % 2 == 0 else 1
    middle = 2 if ep_size % (2 * inner) == 0 else 1
    outer = ep_size // (inner * middle)
    stages = [
        ("ep", inner * middle, outer),
        ("dp", 1, lax.axis_size("dp")),
        ("ep", inner, middle),
        ("ep", 1, inner),
    ]
    return [stage for stage in stages if stage[2] > 1]


def attention_body(
    number_ref, length_ref, q_ref, packed_ref, suffix_ref, *refs, heads, together, aliased
):
    o_ref, k_ref, tail_ref, rotary_ref, bias_ref, sem = refs[aliased:]
    tokens = q_ref.shape[0]
    steps, rows, _ = k_ref.shape
    prefix = steps * rows
    slabs = LATENT // LANES
    factor = score_scale * math.log2(math.e)

    @pl.when(pl.program_id(0) == 0)
    def load_keys():
        copies = []
        for t in range(slabs):
            copies.append(
                pltpu.make_async_copy(
                    packed_ref.at[:, pl.ds(t * rows, rows)],
                    k_ref.at[:, :, pl.ds(t * LANES, LANES)],
                    sem.at[t],
                )
            )
        last = packed_ref.at[:, pl.ds(slabs * rows, rows // 2)]
        copies.append(pltpu.make_async_copy(last, rotary_ref, sem.at[slabs]))
        copies.append(pltpu.make_async_copy(suffix_ref, tail_ref, sem.at[slabs + 1]))
        for copy in copies:
            copy.start()
        lane = lax.broadcasted_iota(jnp.int32, (1, 2 * PAGE), 1)
        for pair in range(prefix // (2 * PAGE)):
            low = number_ref[2 * pair] * PAGE
            high = number_ref[2 * pair + 1] * PAGE - PAGE
            position = lane + jnp.where(lane < PAGE, low, high)
            seen = jnp.where(position < length_ref[0], 0.0, neg_large)
            bias_ref[:, 2 * PAGE * pair : 2 * PAGE * (pair + 1)] = seen.astype(jnp.float32)
        for copy in copies:
            copy.wait()
        for n in range(steps):
            both = rotary_ref[n]
            k_ref[n, : rows // 2, LATENT:] = both[:, : LANES - ROPE]
            k_ref[n, rows // 2 :, LATENT:] = both[:, LANES - ROPE :]

    bias = bias_ref[...]
    suffix = tail_ref.shape[0]
    row = lax.broadcasted_iota(jnp.int32, (tokens, suffix), 0)
    col = lax.broadcasted_iota(jnp.int32, (tokens, suffix), 1)
    causal = jnp.where(col <= row, 0.0, neg_large).astype(jnp.float32)
    causal = jnp.concatenate([causal] * together, axis=0)
    keys = jnp.concatenate([k_ref[...].reshape(prefix, KEY), tail_ref[...]], axis=0)
    for first in range(0, heads, together):
        group = range(first, first + together)
        q = jnp.concatenate([q_ref[:, h * KEY : (h + 1) * KEY] for h in group], axis=0)
        s = lax.dot_general(
            q, keys, (((1,), (1,)), ((), ())), preferred_element_type=jnp.float32
        )
        sp = s[:, :prefix] + bias
        ss = s[:, prefix:] + causal
        m = jnp.maximum(jnp.max(sp, axis=1, keepdims=True), jnp.max(ss, axis=1, keepdims=True))
        shift = m * factor
        pp = jnp.exp2(sp * factor - shift)
        ps = jnp.exp2(ss * factor - shift)
        total = jnp.sum(pp, axis=1, keepdims=True) + jnp.sum(ps, axis=1, keepdims=True)
        p = jnp.concatenate([pp.astype(jnp.bfloat16), ps.astype(jnp.bfloat16)], axis=1)
        acc = jnp.dot(p, keys[:, :LATENT], preferred_element_type=jnp.float32) / total
        for n, h in enumerate(group):
            part = acc[n * tokens : (n + 1) * tokens]
            o_ref[:, h * LATENT : (h + 1) * LATENT] = part.astype(jnp.bfloat16)


def attend(queries, packed, suffix, numbers, length, start, count, heads, so_far=None):
    tokens = queries.shape[0]
    head_count = queries.shape[1] // KEY
    prefix = numbers.shape[0] * PAGE
    steps = packed.shape[0]
    rows = prefix // steps
    scalars = pl.BlockSpec(memory_space=pltpu.SMEM)
    together = 4 if heads % 4 == 0 and prefix <= 2048 else 2
    offset = start // heads
    aliased = 0 if so_far is None else 1
    anywhere = pl.BlockSpec(memory_space=pl.ANY)
    extra = [so_far] if aliased else []
    return pl.pallas_call(
        functools.partial(attention_body, heads=heads, together=together, aliased=aliased),
        grid=(count // heads,),
        in_specs=[
            scalars,
            scalars,
            pl.BlockSpec((tokens, heads * KEY), lambda i: (0, i + offset)),
            *[anywhere] * (2 + aliased),
        ],
        out_specs=pl.BlockSpec((tokens, heads * LATENT), lambda i: (0, i + offset)),
        out_shape=jax.ShapeDtypeStruct((tokens, head_count * LATENT), jnp.bfloat16),
        scratch_shapes=[
            pltpu.VMEM((steps, rows, KEY), jnp.bfloat16),
            pltpu.VMEM(suffix.shape, jnp.bfloat16),
            pltpu.VMEM((steps, rows // 2, LANES), jnp.bfloat16),
            pltpu.VMEM((1, prefix), jnp.float32),
            pltpu.SemaphoreType.DMA((LATENT // LANES + 2,)),
        ],
        input_output_aliases={5: 0} if aliased else {},
        compiler_params=pltpu.CompilerParams(vmem_limit_bytes=58 << 20),
        name="attend",
    )(numbers, length, queries, packed, suffix, *extra)


def fetch_pages(page_pool, page_owner, page_slot):
    ep_size = lax.axis_size("ep")
    pages = page_owner.shape[1]
    ranks = (pages + ep_size - 1) // ep_size
    page_id = jnp.arange(pages, dtype=jnp.int32)
    owners = jnp.arange(ep_size, dtype=jnp.int32)
    rank_id = jnp.arange(ranks, dtype=jnp.int32)
    match = (page_owner[0][None, None, :] == owners[:, None, None]) & (
        page_id[None, None, :] // ep_size == rank_id[None, :, None]
    )
    wanted = jnp.sum(jnp.where(match, page_slot[0][None, None, :], 0), axis=2)
    place = jnp.arange(ep_size * ranks, dtype=jnp.int32)
    seat = page_owner[0] * ranks + page_id // ep_size
    hit = place[:, None] == seat[None, :]
    numbers = pages + jnp.sum(jnp.where(hit, page_id[None, :] - pages, 0), axis=1)
    asked = lax.all_to_all(wanted, "ep", split_axis=0, concat_axis=0, tiled=True)
    pool = page_pool.reshape(page_pool.shape[0], PAGE, KEY)
    chosen = pick_pages(asked, pool)
    fetched = lax.all_to_all(chosen, "ep", split_axis=0, concat_axis=0, tiled=True)
    return fetched, numbers


def pick_body(asked_ref, pool_ref, out_ref):
    steps, ranks = asked_ref.shape
    rows = ranks * PAGE
    slabs = LATENT // LANES
    for n in range(steps):
        rotary = []
        for r in range(ranks):
            page = pool_ref[asked_ref[n, r]]
            for t in range(slabs):
                start = t * rows + r * PAGE
                out_ref[n, start : start + PAGE] = page[:, t * LANES : (t + 1) * LANES]
            rotary.append(page[:, LATENT:])
        rotary = jnp.concatenate(rotary, axis=0)
        low, high = rotary[: rows // 2], rotary[rows // 2 :]
        out_ref[n, slabs * rows :] = jnp.concatenate([low, high], axis=1)


def pick_pages(asked, pool):
    steps, ranks = asked.shape
    whole = pl.BlockSpec(memory_space=pltpu.VMEM)
    return pl.pallas_call(
        pick_body,
        in_specs=[pl.BlockSpec(memory_space=pltpu.SMEM), whole],
        out_specs=whole,
        out_shape=jax.ShapeDtypeStruct((steps, ranks * PAGE * KEY // LANES, LANES), pool.dtype),
        name="pick",
    )(asked, pool)


def split_exact(values):
    high = values.astype(jnp.bfloat16)
    rest = values - high.astype(jnp.float32)
    mid = rest.astype(jnp.bfloat16)
    low = (rest - mid.astype(jnp.float32)).astype(jnp.bfloat16)
    return jnp.concatenate([high, mid, low], axis=1)


def experts_staged(moe_input, expert_ids, gate_weights, w_gate, w_up, w_down):
    ep_size = lax.axis_size("ep")
    _, features = moe_input.shape
    experts = jnp.arange(ep_size, dtype=jnp.int32)
    named = expert_ids[:, :, None] == experts[None, None, :]
    dense = jnp.sum(jnp.where(named, gate_weights[:, :, None], 0.0), axis=1)
    extra = split_exact(dense)
    lanes = -(-extra.shape[1] // 128) * 128
    extra = jnp.pad(extra, ((0, 0), (0, lanes - extra.shape[1])))
    rows = jnp.concatenate([moe_input, extra], axis=1)
    stages = gather_stages()
    for axis, stride, size in stages:
        rows = jnp.concatenate(
            [rows] + [pull(rows, axis, stride, size, shift) for shift in range(1, size)], axis=0
        )
    inputs = rows[:, :features]
    parts = rows[:, features : features + 3 * ep_size].astype(jnp.float32)
    parts = parts.reshape(-1, 3, ep_size)
    here = (experts == lax.axis_index("ep"))[None, None, :]
    parts = jnp.sum(jnp.where(here, parts, 0.0), axis=2)
    weight = (parts[:, 0] + parts[:, 1] + parts[:, 2])[:, None]
    gate_proj = jnp.dot(inputs, w_gate[0], preferred_element_type=jnp.float32)
    up_proj = jnp.dot(inputs, w_up[0], preferred_element_type=jnp.float32)
    hidden = (jax.nn.silu(gate_proj) * up_proj).astype(jnp.bfloat16)
    kept = jnp.dot(hidden, w_down[0], preferred_element_type=jnp.float32) * weight
    for axis, stride, size in reversed(stages):
        count = kept.shape[0] // size
        moved = [
            push(kept[s * count : (s + 1) * count].astype(jnp.bfloat16), axis, stride, size, s)
            for s in range(1, size)
        ]
        kept = kept[:count]
        for m in moved:
            kept = kept + m.astype(jnp.float32)
    return kept.astype(jnp.bfloat16)


def expert_body(me_ref, *refs, places, hidden_steps, experts, features):
    pieces = refs[: len(places)]
    gate_ref, up_ref, down_ref, keep_ref, send_ref, x_ref, h_ref, w_ref, sem = refs[len(places) :]
    step = pl.program_id(0)

    @pl.when(step == 0)
    def load_rows():
        copies = []
        for n, (piece, (row, lane)) in enumerate(zip(pieces, places, strict=True)):
            rows, lanes = piece.shape
            copies.append(
                pltpu.make_async_copy(
                    piece, x_ref.at[pl.ds(row, rows), pl.ds(lane, lanes)], sem.at[n]
                )
            )
        for copy in copies:
            copy.start()
        for copy in copies:
            copy.wait()
        tags = x_ref[:, features:].astype(jnp.float32)
        lane = lax.broadcasted_iota(jnp.int32, tags.shape, 1)
        mine = (lane % experts == me_ref[0]) & (lane < 3 * experts)
        w_ref[...] = jnp.sum(jnp.where(mine, tags, 0.0), axis=1, keepdims=True)

    block = gate_ref.shape[1]
    for n in range(hidden_steps):

        @pl.when(step == n)
        def first_layer(n=n):
            x = x_ref[:, :features]
            gate = jnp.dot(x, gate_ref[...], preferred_element_type=jnp.float32)
            up = jnp.dot(x, up_ref[...], preferred_element_type=jnp.float32)
            hidden = gate / (1.0 + jnp.exp(-gate)) * up
            h_ref[:, n * block : (n + 1) * block] = hidden.astype(jnp.bfloat16)

    @pl.when(step >= hidden_steps)
    def second_layer():
        part = jnp.dot(h_ref[...], down_ref[...], preferred_element_type=jnp.float32)
        total = part * w_ref[...]
        half = keep_ref.shape[0]
        keep_ref[...] = total[:half]
        send_ref[...] = total[half:].astype(jnp.bfloat16)


def expert_call(me, pieces, places, rows, experts, w_gate, w_up, w_down):
    features, hidden = w_gate.shape
    width = pieces[0].shape[1]
    block = 256
    wide = 512 if features % 512 == 0 else 128
    steps = hidden // block
    anywhere = pl.BlockSpec(memory_space=pl.ANY)
    outs = pl.BlockSpec((rows // 2, wide), lambda i: (0, jnp.maximum(i - steps, 0)))
    return pl.pallas_call(
        functools.partial(
            expert_body, places=places, hidden_steps=steps, experts=experts, features=features
        ),
        grid=(steps + features // wide,),
        in_specs=[
            pl.BlockSpec(memory_space=pltpu.SMEM),
            *[anywhere] * len(pieces),
            pl.BlockSpec((features, block), lambda i: (0, jnp.minimum(i, steps - 1))),
            pl.BlockSpec((features, block), lambda i: (0, jnp.minimum(i, steps - 1))),
            pl.BlockSpec((hidden, wide), lambda i: (0, jnp.maximum(i - steps, 0))),
        ],
        out_specs=[outs, outs],
        out_shape=[
            jax.ShapeDtypeStruct((rows // 2, features), jnp.float32),
            jax.ShapeDtypeStruct((rows // 2, features), jnp.bfloat16),
        ],
        scratch_shapes=[
            pltpu.VMEM((rows, width), jnp.bfloat16),
            pltpu.VMEM((rows, hidden), jnp.bfloat16),
            pltpu.VMEM((rows, 1), jnp.float32),
            pltpu.SemaphoreType.DMA((len(pieces),)),
        ],
        compiler_params=pltpu.CompilerParams(vmem_limit_bytes=58 << 20),
        name="expert",
    )(me, *pieces, w_gate, w_up, w_down)


def can_square(tokens, hidden):
    ep_size = lax.axis_size("ep")
    total = tokens * ep_size * lax.axis_size("dp")
    return lax.axis_size("dp") == 2 and ep_size % 4 == 0 and total <= 512 and hidden % 256 == 0


def experts_square(moe_input, expert_ids, gate_weights, w_gate, w_up, w_down):
    ep_size = lax.axis_size("ep")
    outer = ep_size // 4
    tokens, features = moe_input.shape
    left = features // 256 * 128
    experts = jnp.arange(ep_size, dtype=jnp.int32)
    named = expert_ids[:, :, None] == experts[None, None, :]
    dense = jnp.sum(jnp.where(named, gate_weights[:, :, None], 0.0), axis=1)
    extra = split_exact(dense)
    lanes = -(-extra.shape[1] // 128) * 128
    extra = jnp.pad(extra, ((0, 0), (0, lanes - extra.shape[1])))
    rows = jnp.concatenate([moe_input, extra], axis=1)
    far = []
    for shift in range(1, outer):
        far.append(pull(rows, "ep", 4, outer, shift))
    own = jnp.concatenate([rows] + far, axis=0)
    by_x = pull(own, "dp", 1, 2, 1)
    by_y = pull(own, "ep", 2, 2, 1)
    both_a = pull(by_x[:, :left], "ep", 2, 2, 1)
    both_b = pull(by_y[:, left:], "dp", 1, 2, 1)
    near = [own, by_x, by_y, both_a, both_b]
    across = []
    for piece in near:
        across.append(pull(piece, "ep", 1, 2, 1))
    block = own.shape[0]
    places = []
    for base in (0, 4 * block):
        places += [(base + n * block, 0) for n in range(3)]
        places += [(base + 3 * block, 0), (base + 3 * block, left)]
    me = lax.axis_index("ep").astype(jnp.int32).reshape(1)
    keep, send = expert_call(
        me, near + across, tuple(places), 8 * block, ep_size, w_gate[0], w_up[0], w_down[0]
    )
    got = pull(send, "ep", 1, 2, 1)
    yield None
    keep = keep + got.astype(jnp.float32)
    own, by_x, by_y, both = (keep[n * block : (n + 1) * block] for n in range(4))
    got_a = pull(both[:, :left].astype(jnp.bfloat16), "ep", 2, 2, 1)
    got_b = pull(both[:, left:].astype(jnp.bfloat16), "dp", 1, 2, 1)
    yield None
    by_x = jnp.concatenate([by_x[:, :left] + got_a.astype(jnp.float32), by_x[:, left:]], axis=1)
    by_y = jnp.concatenate([by_y[:, :left], by_y[:, left:] + got_b.astype(jnp.float32)], axis=1)
    got_x = pull(by_x.astype(jnp.bfloat16), "dp", 1, 2, 1)
    got_y = pull(by_y.astype(jnp.bfloat16), "ep", 2, 2, 1)
    yield None
    own = own + got_x.astype(jnp.float32) + got_y.astype(jnp.float32)
    got = []
    for shift in range(1, outer):
        piece = own[shift * tokens : (shift + 1) * tokens].astype(jnp.bfloat16)
        got.append(push(piece, "ep", 4, outer, shift))
    yield None
    total = own[:tokens]
    for piece in got:
        total = total + piece.astype(jnp.float32)
    yield total.astype(jnp.bfloat16)


def on_device(
    queries,
    suffix_latent,
    page_pool,
    page_owner,
    page_slot,
    prefix_len,
    moe_input,
    expert_ids,
    gate_weights,
    w_gate,
    w_up,
    w_down,
):
    packed, numbers = fetch_pages(page_pool, page_owner, page_slot)
    source = (queries, packed, suffix_latent, numbers, prefix_len)
    moe_args = (moe_input, expert_ids, gate_weights, w_gate, w_up, w_down)
    head_count = queries.shape[1] // KEY
    if not can_square(moe_input.shape[0], w_gate.shape[2]):
        moe_output = experts_staged(*moe_args)
        return (attend(*source, 0, head_count, 2), moe_output)
    stages = experts_square(*moe_args)
    heads = 4
    steps = head_count // heads
    next(stages)
    cuts = [0, steps // 4, 5 * steps // 8, steps]
    attn_context = None
    for n in range(3):
        next(stages)
        start, count = cuts[n] * heads, (cuts[n + 1] - cuts[n]) * heads
        if count:
            attn_context = attend(*source, start, count, heads, attn_context)
    moe_output = next(stages)
    return (attn_context, moe_output)


def solution(mesh):
    return jax.shard_map(
        on_device,
        mesh=mesh,
        in_specs=(
            P("ep", "dp"),
            P("ep", None),
            P("ep", None),
            P("ep", None),
            P("ep", None),
            P("ep"),
            P(("dp", "ep"), None),
            P(("dp", "ep"), None),
            P(("dp", "ep"), None),
            P("ep", None, "dp"),
            P("ep", None, "dp"),
            P("ep", "dp", None),
        ),
        out_specs=(P("ep", "dp"), P(("dp", "ep"), None)),
        check_vma=False,
    )
```

```python
import functools
import math

import jax
import jax.numpy as jnp
from jax import lax
from jax.experimental import pallas as pl
from jax.experimental.pallas import tpu as pltpu
from jax.sharding import PartitionSpec as P


LATENT = 512
ROPE = 64
KEY = LATENT + ROPE
PAGE = 64

score_scale = 0.07216878364870322
neg_large = -1e30


def partner(pos, shift, size):
    return pos ^ shift if size & (size - 1) == 0 else (pos + shift) % size


def pull(values, axis, stride, size, shift, back=False):
    total = lax.axis_size(axis)
    pairs = []
    for dst in range(total):
        pos = (dst // stride) % size
        src = dst + (partner(pos, shift, size) - pos) * stride
        pairs.append((dst, src) if back else (src, dst))
    return lax.ppermute(values, axis, pairs)


def push(values, axis, stride, size, shift):
    return pull(values, axis, stride, size, shift, back=True)


def gather_stages():
    ep_size = lax.axis_size("ep")
    inner = 2 if ep_size % 2 == 0 else 1
    middle = 2 if ep_size % (2 * inner) == 0 else 1
    outer = ep_size // (inner * middle)
    stages = [
        ("ep", inner * middle, outer),
        ("dp", 1, lax.axis_size("dp")),
        ("ep", inner, middle),
        ("ep", 1, inner),
    ]
    return [stage for stage in stages if stage[2] > 1]


def attention_body(
    number_ref, length_ref, q_ref, *refs, heads, together, count, aliased
):
    pieces = refs[:count]
    o_ref, k_ref, bias_ref, sem = refs[count + aliased :]
    tokens = q_ref.shape[0]
    prefix = bias_ref.shape[1]
    factor = score_scale * math.log2(math.e)

    @pl.when(pl.program_id(0) == 0)
    def load_keys():
        copies = []
        start = 0
        for n, piece in enumerate(pieces):
            rows = piece.shape[0]
            copies.append(
                pltpu.make_async_copy(piece, k_ref.at[pl.ds(start, rows)], sem.at[n])
            )
            start += rows
        for copy in copies:
            copy.start()
        lane = lax.broadcasted_iota(jnp.int32, (1, 2 * PAGE), 1)
        for pair in range(prefix // (2 * PAGE)):
            low = number_ref[2 * pair] * PAGE
            high = number_ref[2 * pair + 1] * PAGE - PAGE
            position = lane + jnp.where(lane < PAGE, low, high)
            seen = jnp.where(position < length_ref[0], 0.0, neg_large)
            bias_ref[:, 2 * PAGE * pair : 2 * PAGE * (pair + 1)] = seen.astype(jnp.float32)
        for copy in copies:
            copy.wait()

    bias = bias_ref[...]
    suffix = k_ref.shape[0] - prefix
    row = lax.broadcasted_iota(jnp.int32, (tokens, suffix), 0)
    col = lax.broadcasted_iota(jnp.int32, (tokens, suffix), 1)
    causal = jnp.where(col <= row, 0.0, neg_large).astype(jnp.float32)
    causal = jnp.concatenate([causal] * together, axis=0)
    for first in range(0, heads, together):
        group = range(first, first + together)
        q = jnp.concatenate([q_ref[:, h * KEY : (h + 1) * KEY] for h in group], axis=0)
        s = lax.dot_general(
            q, k_ref[...], (((1,), (1,)), ((), ())), preferred_element_type=jnp.float32
        )
        sp = s[:, :prefix] + bias
        ss = s[:, prefix:] + causal
        m = jnp.maximum(jnp.max(sp, axis=1, keepdims=True), jnp.max(ss, axis=1, keepdims=True))
        shift = m * factor
        pp = jnp.exp2(sp * factor - shift)
        ps = jnp.exp2(ss * factor - shift)
        total = jnp.sum(pp, axis=1, keepdims=True) + jnp.sum(ps, axis=1, keepdims=True)
        p = jnp.concatenate([pp.astype(jnp.bfloat16), ps.astype(jnp.bfloat16)], axis=1)
        acc = jnp.dot(p, k_ref[:, :LATENT], preferred_element_type=jnp.float32) / total
        for n, h in enumerate(group):
            part = acc[n * tokens : (n + 1) * tokens]
            o_ref[:, h * LATENT : (h + 1) * LATENT] = part.astype(jnp.bfloat16)


def attend(queries, pieces, numbers, length, start, count, heads, so_far=None):
    tokens = queries.shape[0]
    head_count = queries.shape[1] // KEY
    prefix = numbers.shape[0] * PAGE
    keys = sum(piece.shape[0] for piece in pieces)
    scalars = pl.BlockSpec(memory_space=pltpu.SMEM)
    together = 4 if heads % 4 == 0 and prefix <= 2048 else 2
    offset = start // heads
    aliased = 0 if so_far is None else 1
    anywhere = pl.BlockSpec(memory_space=pl.ANY)
    extra = [so_far] if aliased else []
    return pl.pallas_call(
        functools.partial(
            attention_body, heads=heads, together=together, count=len(pieces), aliased=aliased
        ),
        grid=(count // heads,),
        in_specs=[
            scalars,
            scalars,
            pl.BlockSpec((tokens, heads * KEY), lambda i: (0, i + offset)),
            *[anywhere] * (len(pieces) + aliased),
        ],
        out_specs=pl.BlockSpec((tokens, heads * LATENT), lambda i: (0, i + offset)),
        out_shape=jax.ShapeDtypeStruct((tokens, head_count * LATENT), jnp.bfloat16),
        scratch_shapes=[
            pltpu.VMEM((keys, KEY), jnp.bfloat16),
            pltpu.VMEM((1, prefix), jnp.float32),
            pltpu.SemaphoreType.DMA((len(pieces),)),
        ],
        input_output_aliases={3 + len(pieces): 0} if aliased else {},
        compiler_params=pltpu.CompilerParams(vmem_limit_bytes=58 << 20),
        name="attend",
    )(numbers, length, queries, *pieces, *extra)


def fetch_pages(page_pool, page_owner, page_slot):
    ep_size = lax.axis_size("ep")
    me = lax.axis_index("ep").astype(jnp.int32)
    pages = page_owner.shape[1]
    ranks = (pages + ep_size - 1) // ep_size
    inner = 4 if ep_size % 4 == 0 else 1
    outer = ep_size // inner
    pool = page_pool.reshape(page_pool.shape[0], PAGE, KEY)
    pools = [pool]
    for a in range(1, outer):
        pools.append(pull(pool, "ep", inner, outer, a))
    table = jnp.concatenate([page_owner, page_slot], axis=0)
    tables = [table]
    for b in range(1, inner):
        tables.append(push(table, "ep", 1, inner, b))
    cuts = sorted({0, outer // 2, outer})
    pieces = []
    group, place = me // inner, me % inner
    owners = []
    for low, high in zip(cuts, cuts[1:]):
        hosts = [partner(group, jnp.int32(a), outer) * inner + place for a in range(low, high)]
        parts = pick_pages(jnp.stack(hosts), tables, pools[low:high], ep_size, ranks)
        for b in range(inner):
            pieces.append(pull(parts[b], "ep", 1, inner, b) if b else parts[b])
            owners += [(a, b) for a in range(low, high)]
    across = jnp.array([a for a, _ in owners], jnp.int32)
    beside = jnp.array([b for _, b in owners], jnp.int32)
    hear = partner(group, across, outer) * inner + partner(place, beside, inner)
    page_id = jnp.arange(pages, dtype=jnp.int32)
    seat = page_owner[0] * ranks + page_id // ep_size
    place_of = hear[:, None] * ranks + jnp.arange(ranks, dtype=jnp.int32)[None, :]
    hit = place_of.reshape(-1, 1) == seat[None, :]
    numbers = pages + jnp.sum(jnp.where(hit, page_id[None, :] - pages, 0), axis=1)
    return pieces, numbers


def pick_body(host_ref, *refs, count, total, ep_size, ranks):
    inner = (len(refs) - 1 - count) // 2
    tables = refs[:inner]
    pools = refs[inner : inner + count]
    outs = refs[inner + count : -1]
    slot_ref = refs[-1]
    for b, table in enumerate(tables):
        if total != ep_size * ranks:
            for n in range(ep_size * ranks):
                slot_ref[b, n] = 0
        for k in range(table.shape[1]):
            slot_ref[b, table[0, k] * ranks + k // ep_size] = table[1, k]
        for n, pool in enumerate(pools):
            for r in range(ranks):
                slot = slot_ref[b, host_ref[n] * ranks + r]
                start = (n * ranks + r) * PAGE
                outs[b][start : start + PAGE] = pool[slot]


def pick_pages(hosts, tables, pools, ep_size, ranks):
    rows = len(pools) * ranks * PAGE
    scalars = pl.BlockSpec(memory_space=pltpu.SMEM)
    whole = pl.BlockSpec(memory_space=pltpu.VMEM)
    total = tables[0].shape[1]
    return pl.pallas_call(
        functools.partial(
            pick_body, count=len(pools), total=total, ep_size=ep_size, ranks=ranks
        ),
        in_specs=[scalars] * (1 + len(tables)) + [whole] * len(pools),
        out_specs=[whole] * len(tables),
        out_shape=[jax.ShapeDtypeStruct((rows, KEY), pools[0].dtype)] * len(tables),
        scratch_shapes=[pltpu.SMEM((len(tables), ep_size * ranks), jnp.int32)],
        name="pick",
    )(hosts, *tables, *pools)


def split_exact(values):
    high = values.astype(jnp.bfloat16)
    rest = values - high.astype(jnp.float32)
    mid = rest.astype(jnp.bfloat16)
    low = (rest - mid.astype(jnp.float32)).astype(jnp.bfloat16)
    return jnp.concatenate([high, mid, low], axis=1)


def experts_staged(moe_input, expert_ids, gate_weights, w_gate, w_up, w_down):
    ep_size = lax.axis_size("ep")
    _, features = moe_input.shape
    experts = jnp.arange(ep_size, dtype=jnp.int32)
    named = expert_ids[:, :, None] == experts[None, None, :]
    dense = jnp.sum(jnp.where(named, gate_weights[:, :, None], 0.0), axis=1)
    extra = split_exact(dense)
    lanes = -(-extra.shape[1] // 128) * 128
    extra = jnp.pad(extra, ((0, 0), (0, lanes - extra.shape[1])))
    rows = jnp.concatenate([moe_input, extra], axis=1)
    stages = gather_stages()
    for axis, stride, size in stages:
        rows = jnp.concatenate(
            [rows] + [pull(rows, axis, stride, size, shift) for shift in range(1, size)], axis=0
        )
    inputs = rows[:, :features]
    parts = rows[:, features : features + 3 * ep_size].astype(jnp.float32)
    parts = parts.reshape(-1, 3, ep_size)
    here = (experts == lax.axis_index("ep"))[None, None, :]
    parts = jnp.sum(jnp.where(here, parts, 0.0), axis=2)
    weight = (parts[:, 0] + parts[:, 1] + parts[:, 2])[:, None]
    gate_proj = jnp.dot(inputs, w_gate[0], preferred_element_type=jnp.float32)
    up_proj = jnp.dot(inputs, w_up[0], preferred_element_type=jnp.float32)
    hidden = (jax.nn.silu(gate_proj) * up_proj).astype(jnp.bfloat16)
    kept = jnp.dot(hidden, w_down[0], preferred_element_type=jnp.float32) * weight
    for axis, stride, size in reversed(stages):
        count = kept.shape[0] // size
        moved = [
            push(kept[s * count : (s + 1) * count].astype(jnp.bfloat16), axis, stride, size, s)
            for s in range(1, size)
        ]
        kept = kept[:count]
        for m in moved:
            kept = kept + m.astype(jnp.float32)
    return kept.astype(jnp.bfloat16)


def expert_body(me_ref, *refs, places, hidden_steps, experts, features):
    pieces = refs[: len(places)]
    gate_ref, up_ref, down_ref, keep_ref, send_ref, x_ref, h_ref, w_ref, sem = refs[len(places) :]
    step = pl.program_id(0)

    @pl.when(step == 0)
    def load_rows():
        copies = []
        for n, (piece, (row, lane)) in enumerate(zip(pieces, places, strict=True)):
            rows, lanes = piece.shape
            copies.append(
                pltpu.make_async_copy(
                    piece, x_ref.at[pl.ds(row, rows), pl.ds(lane, lanes)], sem.at[n]
                )
            )
        for copy in copies:
            copy.start()
        for copy in copies:
            copy.wait()
        tags = x_ref[:, features:].astype(jnp.float32)
        lane = lax.broadcasted_iota(jnp.int32, tags.shape, 1)
        mine = (lane % experts == me_ref[0]) & (lane < 3 * experts)
        w_ref[...] = jnp.sum(jnp.where(mine, tags, 0.0), axis=1, keepdims=True)

    block = gate_ref.shape[1]
    for n in range(hidden_steps):

        @pl.when(step == n)
        def first_layer(n=n):
            x = x_ref[:, :features]
            gate = jnp.dot(x, gate_ref[...], preferred_element_type=jnp.float32)
            up = jnp.dot(x, up_ref[...], preferred_element_type=jnp.float32)
            hidden = gate / (1.0 + jnp.exp(-gate)) * up
            h_ref[:, n * block : (n + 1) * block] = hidden.astype(jnp.bfloat16)

    @pl.when(step >= hidden_steps)
    def second_layer():
        part = jnp.dot(h_ref[...], down_ref[...], preferred_element_type=jnp.float32)
        total = part * w_ref[...]
        half = keep_ref.shape[0]
        keep_ref[...] = total[:half]
        send_ref[...] = total[half:].astype(jnp.bfloat16)


def expert_call(me, pieces, places, rows, experts, w_gate, w_up, w_down):
    features, hidden = w_gate.shape
    width = pieces[0].shape[1]
    block = 256
    wide = 512 if features % 512 == 0 else 128
    steps = hidden // block
    anywhere = pl.BlockSpec(memory_space=pl.ANY)
    outs = pl.BlockSpec((rows // 2, wide), lambda i: (0, jnp.maximum(i - steps, 0)))
    return pl.pallas_call(
        functools.partial(
            expert_body, places=places, hidden_steps=steps, experts=experts, features=features
        ),
        grid=(steps + features // wide,),
        in_specs=[
            pl.BlockSpec(memory_space=pltpu.SMEM),
            *[anywhere] * len(pieces),
            pl.BlockSpec((features, block), lambda i: (0, jnp.minimum(i, steps - 1))),
            pl.BlockSpec((features, block), lambda i: (0, jnp.minimum(i, steps - 1))),
            pl.BlockSpec((hidden, wide), lambda i: (0, jnp.maximum(i - steps, 0))),
        ],
        out_specs=[outs, outs],
        out_shape=[
            jax.ShapeDtypeStruct((rows // 2, features), jnp.float32),
            jax.ShapeDtypeStruct((rows // 2, features), jnp.bfloat16),
        ],
        scratch_shapes=[
            pltpu.VMEM((rows, width), jnp.bfloat16),
            pltpu.VMEM((rows, hidden), jnp.bfloat16),
            pltpu.VMEM((rows, 1), jnp.float32),
            pltpu.SemaphoreType.DMA((len(pieces),)),
        ],
        compiler_params=pltpu.CompilerParams(vmem_limit_bytes=58 << 20),
        name="expert",
    )(me, *pieces, w_gate, w_up, w_down)


def can_square(tokens, hidden):
    ep_size = lax.axis_size("ep")
    total = tokens * ep_size * lax.axis_size("dp")
    return lax.axis_size("dp") == 2 and ep_size % 4 == 0 and total <= 512 and hidden % 256 == 0


def experts_square(moe_input, expert_ids, gate_weights, w_gate, w_up, w_down):
    ep_size = lax.axis_size("ep")
    outer = ep_size // 4
    tokens, _ = moe_input.shape
    experts = jnp.arange(ep_size, dtype=jnp.int32)
    named = expert_ids[:, :, None] == experts[None, None, :]
    dense = jnp.sum(jnp.where(named, gate_weights[:, :, None], 0.0), axis=1)
    extra = split_exact(dense)
    lanes = -(-extra.shape[1] // 128) * 128
    extra = jnp.pad(extra, ((0, 0), (0, lanes - extra.shape[1])))
    rows = jnp.concatenate([moe_input, extra], axis=1)
    far = []
    for shift in range(1, outer):
        far.append(pull(rows, "ep", 4, outer, shift))
    own = jnp.concatenate([rows] + far, axis=0)
    by_x = pull(own, "dp", 1, 2, 1)
    by_y = pull(own, "ep", 2, 2, 1)
    both = pull(by_y, "dp", 1, 2, 1)
    near = [own, by_x, by_y, both]
    across = []
    for piece in near:
        across.append(pull(piece, "ep", 1, 2, 1))
    block = own.shape[0]
    places = [(n * block, 0) for n in range(8)]
    me = lax.axis_index("ep").astype(jnp.int32).reshape(1)
    keep, send = expert_call(
        me, near + across, tuple(places), 8 * block, ep_size, w_gate[0], w_up[0], w_down[0]
    )
    got = pull(send, "ep", 1, 2, 1)
    yield None
    keep = keep + got.astype(jnp.float32)
    own, by_x, by_y, both = (keep[n * block : (n + 1) * block] for n in range(4))
    got_both = pull(both.astype(jnp.bfloat16), "dp", 1, 2, 1)
    got_x = pull(by_x.astype(jnp.bfloat16), "dp", 1, 2, 1)
    yield None
    by_y = by_y + got_both.astype(jnp.float32)
    got_y = pull(by_y.astype(jnp.bfloat16), "ep", 2, 2, 1)
    yield None
    own = own + got_x.astype(jnp.float32) + got_y.astype(jnp.float32)
    got = []
    for shift in range(1, outer):
        piece = own[shift * tokens : (shift + 1) * tokens].astype(jnp.bfloat16)
        got.append(push(piece, "ep", 4, outer, shift))
    yield None
    total = own[:tokens]
    for piece in got:
        total = total + piece.astype(jnp.float32)
    yield total.astype(jnp.bfloat16)


def on_device(
    queries,
    suffix_latent,
    page_pool,
    page_owner,
    page_slot,
    prefix_len,
    moe_input,
    expert_ids,
    gate_weights,
    w_gate,
    w_up,
    w_down,
):
    pieces, numbers = fetch_pages(page_pool, page_owner, page_slot)
    source = (queries, pieces + [suffix_latent], numbers, prefix_len)
    moe_args = (moe_input, expert_ids, gate_weights, w_gate, w_up, w_down)
    head_count = queries.shape[1] // KEY
    if not can_square(moe_input.shape[0], w_gate.shape[2]):
        moe_output = experts_staged(*moe_args)
        return (attend(*source, 0, head_count, 2), moe_output)
    stages = experts_square(*moe_args)
    heads = 4
    steps = head_count // heads
    cuts = [0, steps // 8, 3 * steps // 8, 6 * steps // 8, steps]
    attn_context = None
    for n in range(4):
        next(stages)
        start, count = cuts[n] * heads, (cuts[n + 1] - cuts[n]) * heads
        if count:
            attn_context = attend(*source, start, count, heads, attn_context)
    moe_output = next(stages)
    return (attn_context, moe_output)


def solution(mesh):
    return jax.shard_map(
        on_device,
        mesh=mesh,
        in_specs=(
            P("ep", "dp"),
            P("ep", None),
            P("ep", None),
            P("ep", None),
            P("ep", None),
            P("ep"),
            P(("dp", "ep"), None),
            P(("dp", "ep"), None),
            P(("dp", "ep"), None),
            P("ep", None, "dp"),
            P("ep", None, "dp"),
            P("ep", "dp", None),
        ),
        out_specs=(P("ep", "dp"), P(("dp", "ep"), None)),
        check_vma=False,
    )
```

```python
import functools
import math

import jax
import jax.numpy as jnp
from jax import lax
from jax.experimental import pallas as pl
from jax.experimental.pallas import tpu as pltpu
from jax.sharding import PartitionSpec as P


LATENT = 512
ROPE = 64
KEY = LATENT + ROPE
PAGE = 64
LANES = 128

score_scale = 0.07216878364870322
neg_large = -1e30


def partner(pos, shift, size):
    return pos ^ shift if size & (size - 1) == 0 else (pos + shift) % size


def pull(values, axis, stride, size, shift, back=False):
    total = lax.axis_size(axis)
    pairs = []
    for dst in range(total):
        pos = (dst // stride) % size
        src = dst + (partner(pos, shift, size) - pos) * stride
        pairs.append((dst, src) if back else (src, dst))
    return lax.ppermute(values, axis, pairs)


def push(values, axis, stride, size, shift):
    return pull(values, axis, stride, size, shift, back=True)


def gather_stages():
    ep_size = lax.axis_size("ep")
    inner = 2 if ep_size % 2 == 0 else 1
    middle = 2 if ep_size % (2 * inner) == 0 else 1
    outer = ep_size // (inner * middle)
    stages = [
        ("ep", inner * middle, outer),
        ("dp", 1, lax.axis_size("dp")),
        ("ep", inner, middle),
        ("ep", 1, inner),
    ]
    return [stage for stage in stages if stage[2] > 1]


def attention_body(*refs, heads, together, tail, begins, ends, aliased):
    number_ref, length_ref, q_ref, packed_ref, *refs = refs
    if tail:
        suffix_ref, *refs = refs
    if not begins:
        acc_in_ref, state_in_ref, *refs = refs
    refs = refs[aliased:]
    if ends:
        o_ref, *refs = refs
    else:
        acc_ref, state_ref, *refs = refs
    k_ref, page_ref, rotary_ref, bias_ref, sem = refs
    tokens = q_ref.shape[0]
    steps = page_ref.shape[0]
    prefix = steps * PAGE
    slabs = LATENT // LANES
    factor = score_scale * math.log2(math.e)

    @pl.when(pl.program_id(0) == 0)
    def load_keys():
        copies = []
        for t in range(slabs):
            copies.append(
                pltpu.make_async_copy(
                    packed_ref.at[:, pl.ds(t * PAGE, PAGE)],
                    page_ref.at[:, :, pl.ds(t * LANES, LANES)],
                    sem.at[t],
                )
            )
        last = packed_ref.at[:, pl.ds(slabs * PAGE, PAGE // 2)]
        copies.append(pltpu.make_async_copy(last, rotary_ref, sem.at[slabs]))
        if tail:
            copies.append(
                pltpu.make_async_copy(suffix_ref, k_ref.at[pl.ds(prefix, tail)], sem.at[slabs + 1])
            )
        for copy in copies:
            copy.start()
        lane = lax.broadcasted_iota(jnp.int32, (1, 2 * PAGE), 1)
        for pair in range(steps // 2):
            low = number_ref[2 * pair] * PAGE
            high = number_ref[2 * pair + 1] * PAGE - PAGE
            position = lane + jnp.where(lane < PAGE, low, high)
            seen = jnp.where(position < length_ref[0], 0.0, neg_large)
            bias_ref[:, 2 * PAGE * pair : 2 * PAGE * (pair + 1)] = seen.astype(jnp.float32)
        for copy in copies:
            copy.wait()
        half = PAGE // 2
        for n in range(steps):
            start = n * PAGE
            k_ref[start : start + PAGE, :LATENT] = page_ref[n]
            both = rotary_ref[n]
            k_ref[start : start + half, LATENT:] = both[:, :ROPE]
            k_ref[start + half : start + PAGE, LATENT:] = both[:, ROPE:]

    bias = bias_ref[...]
    if tail:
        row = lax.broadcasted_iota(jnp.int32, (tokens, tail), 0)
        col = lax.broadcasted_iota(jnp.int32, (tokens, tail), 1)
        causal = jnp.where(col <= row, 0.0, neg_large).astype(jnp.float32)
        causal = jnp.concatenate([causal] * together, axis=0)
    for first in range(0, heads, together):
        group = range(first, first + together)
        q = jnp.concatenate([q_ref[:, h * KEY : (h + 1) * KEY] for h in group], axis=0)
        s = lax.dot_general(
            q, k_ref[...], (((1,), (1,)), ((), ())), preferred_element_type=jnp.float32
        )
        blocks = [s[:, :prefix] + bias]
        if tail:
            blocks.append(s[:, prefix:] + causal)
        tops = [jnp.max(block, axis=1, keepdims=True) for block in blocks]
        if not begins:
            states = [state_in_ref[:, h * LANES : (h + 1) * LANES] for h in group]
            state = jnp.concatenate(states, axis=0)
            before = state[:, :1]
            tops.append(before)
        m = functools.reduce(jnp.maximum, tops)
        shift = m * factor
        powers = [jnp.exp2(block * factor - shift) for block in blocks]
        total = sum(jnp.sum(power, axis=1, keepdims=True) for power in powers)
        p = jnp.concatenate([power.astype(jnp.bfloat16) for power in powers], axis=1)
        acc = jnp.dot(p, k_ref[:, :LATENT], preferred_element_type=jnp.float32)
        if not begins:
            scale = jnp.exp2(before * factor - shift)
            total = total + state[:, LANES - 1 :] * scale
            olds = [acc_in_ref[:, h * LATENT : (h + 1) * LATENT] for h in group]
            acc = acc + jnp.concatenate(olds, axis=0) * scale
        if ends:
            acc = acc / total
        else:
            lane = lax.broadcasted_iota(jnp.int32, (acc.shape[0], LANES), 1)
            state = jnp.where(lane < LANES // 2, m, total)
        for n, h in enumerate(group):
            rows = slice(n * tokens, (n + 1) * tokens)
            if ends:
                o_ref[:, h * LATENT : (h + 1) * LATENT] = acc[rows].astype(jnp.bfloat16)
            else:
                acc_ref[:, h * LATENT : (h + 1) * LATENT] = acc[rows]
                state_ref[:, h * LANES : (h + 1) * LANES] = state[rows]


def attend(
    queries, packed, suffix, numbers, length, start, count, heads, before=None, ends=True, so_far=None
):
    tokens = queries.shape[0]
    head_count = queries.shape[1] // KEY
    steps = packed.shape[0]
    prefix = steps * PAGE
    begins = before is None
    tail = suffix.shape[0] if begins else 0
    together = 4 if heads % 4 == 0 and prefix <= 2048 else 2
    offset = start // heads
    aliased = 0 if so_far is None else 1
    scalars = pl.BlockSpec(memory_space=pltpu.SMEM)
    anywhere = pl.BlockSpec(memory_space=pl.ANY)
    operands = [numbers, length, queries, packed]
    in_specs = [
        scalars,
        scalars,
        pl.BlockSpec((tokens, heads * KEY), lambda i: (0, i + offset)),
        anywhere,
    ]
    if begins:
        operands.append(suffix)
        in_specs.append(anywhere)
    else:
        operands += before
        in_specs += [
            pl.BlockSpec((tokens, heads * LATENT), lambda i: (0, i)),
            pl.BlockSpec((tokens, heads * LANES), lambda i: (0, i)),
        ]
    if aliased:
        operands.append(so_far)
        in_specs.append(anywhere)
    if ends:
        out_specs = pl.BlockSpec((tokens, heads * LATENT), lambda i: (0, i + offset))
        out_shape = jax.ShapeDtypeStruct((tokens, head_count * LATENT), jnp.bfloat16)
    else:
        out_specs = [
            pl.BlockSpec((tokens, heads * LATENT), lambda i: (0, i)),
            pl.BlockSpec((tokens, heads * LANES), lambda i: (0, i)),
        ]
        out_shape = [
            jax.ShapeDtypeStruct((tokens, count * LATENT), jnp.float32),
            jax.ShapeDtypeStruct((tokens, count * LANES), jnp.float32),
        ]
    return pl.pallas_call(
        functools.partial(
            attention_body,
            heads=heads,
            together=together,
            tail=tail,
            begins=begins,
            ends=ends,
            aliased=aliased,
        ),
        grid=(count // heads,),
        in_specs=in_specs,
        out_specs=out_specs,
        out_shape=out_shape,
        scratch_shapes=[
            pltpu.VMEM((prefix + tail, KEY), jnp.bfloat16),
            pltpu.VMEM((steps, PAGE, LATENT), jnp.bfloat16),
            pltpu.VMEM((steps, PAGE // 2, LANES), jnp.bfloat16),
            pltpu.VMEM((1, prefix), jnp.float32),
            pltpu.SemaphoreType.DMA((LATENT // LANES + 2,)),
        ],
        input_output_aliases={len(operands) - 1: 0} if aliased else {},
        compiler_params=pltpu.CompilerParams(vmem_limit_bytes=58 << 20),
        name="attend",
    )(*operands)


def fetch_pages(page_pool, page_owner, page_slot):
    ep_size = lax.axis_size("ep")
    pages = page_owner.shape[1]
    ranks = (pages + ep_size - 1) // ep_size
    page_id = jnp.arange(pages, dtype=jnp.int32)
    owners = jnp.arange(ep_size, dtype=jnp.int32)
    rank_id = jnp.arange(ranks, dtype=jnp.int32)
    match = (page_owner[0][None, None, :] == owners[:, None, None]) & (
        page_id[None, None, :] // ep_size == rank_id[None, :, None]
    )
    wanted = jnp.sum(jnp.where(match, page_slot[0][None, None, :], 0), axis=2)
    asked = lax.all_to_all(wanted, "ep", split_axis=0, concat_axis=0, tiled=True)
    pool = page_pool.reshape(page_pool.shape[0], PAGE, KEY)
    place = jnp.arange(ep_size, dtype=jnp.int32)

    def number(first):
        low = first * ep_size
        ids = low + jnp.arange(min(ep_size, pages), dtype=jnp.int32)
        held = lax.dynamic_slice_in_dim(page_owner[0], low, min(ep_size, pages))
        hit = place[:, None] == held[None, :]
        return pages + jnp.sum(jnp.where(hit, ids[None, :] - pages, 0), axis=1)

    dp_size = lax.axis_size("dp")
    if ranks == dp_size and pages == ranks * ep_size:
        plane = lax.axis_index("dp").astype(jnp.int32)
        chosen = pick_pages(plane.reshape(1), asked, pool)
        own = lax.all_to_all(chosen, "ep", split_axis=0, concat_axis=0, tiled=True)
        fetched, numbers = [own], [number(plane)]
        for shift in range(1, dp_size):
            fetched.append(pull(own, "dp", 1, dp_size, shift))
            numbers.append(number(partner(plane, jnp.int32(shift), dp_size)))
        return fetched, numbers
    fetched, numbers = [], []
    for r in range(ranks):
        chosen = pick_pages(jnp.full((1,), r, jnp.int32), asked, pool)
        fetched.append(lax.all_to_all(chosen, "ep", split_axis=0, concat_axis=0, tiled=True))
        numbers.append(number(jnp.int32(r)))
    return fetched, numbers


def pick_body(rank_ref, asked_ref, pool_ref, out_ref):
    slabs = LATENT // LANES
    half = PAGE // 2
    for n in range(asked_ref.shape[0]):
        page = pool_ref[asked_ref[n, rank_ref[0]]]
        for t in range(slabs):
            out_ref[n, t * PAGE : (t + 1) * PAGE] = page[:, t * LANES : (t + 1) * LANES]
        rotary = page[:, LATENT:]
        out_ref[n, slabs * PAGE :] = jnp.concatenate([rotary[:half], rotary[half:]], axis=1)


def pick_pages(rank, asked, pool):
    scalars = pl.BlockSpec(memory_space=pltpu.SMEM)
    whole = pl.BlockSpec(memory_space=pltpu.VMEM)
    shape = (asked.shape[0], PAGE * KEY // LANES, LANES)
    return pl.pallas_call(
        pick_body,
        in_specs=[scalars, scalars, whole],
        out_specs=whole,
        out_shape=jax.ShapeDtypeStruct(shape, pool.dtype),
        name="pick",
    )(rank, asked, pool)


def split_exact(values):
    high = values.astype(jnp.bfloat16)
    rest = values - high.astype(jnp.float32)
    mid = rest.astype(jnp.bfloat16)
    low = (rest - mid.astype(jnp.float32)).astype(jnp.bfloat16)
    return jnp.concatenate([high, mid, low], axis=1)


def experts_staged(moe_input, expert_ids, gate_weights, w_gate, w_up, w_down):
    ep_size = lax.axis_size("ep")
    _, features = moe_input.shape
    experts = jnp.arange(ep_size, dtype=jnp.int32)
    named = expert_ids[:, :, None] == experts[None, None, :]
    dense = jnp.sum(jnp.where(named, gate_weights[:, :, None], 0.0), axis=1)
    extra = split_exact(dense)
    lanes = -(-extra.shape[1] // 128) * 128
    extra = jnp.pad(extra, ((0, 0), (0, lanes - extra.shape[1])))
    rows = jnp.concatenate([moe_input, extra], axis=1)
    stages = gather_stages()
    for axis, stride, size in stages:
        rows = jnp.concatenate(
            [rows] + [pull(rows, axis, stride, size, shift) for shift in range(1, size)], axis=0
        )
    inputs = rows[:, :features]
    parts = rows[:, features : features + 3 * ep_size].astype(jnp.float32)
    parts = parts.reshape(-1, 3, ep_size)
    here = (experts == lax.axis_index("ep"))[None, None, :]
    parts = jnp.sum(jnp.where(here, parts, 0.0), axis=2)
    weight = (parts[:, 0] + parts[:, 1] + parts[:, 2])[:, None]
    gate_proj = jnp.dot(inputs, w_gate[0], preferred_element_type=jnp.float32)
    up_proj = jnp.dot(inputs, w_up[0], preferred_element_type=jnp.float32)
    hidden = (jax.nn.silu(gate_proj) * up_proj).astype(jnp.bfloat16)
    kept = jnp.dot(hidden, w_down[0], preferred_element_type=jnp.float32) * weight
    for axis, stride, size in reversed(stages):
        count = kept.shape[0] // size
        moved = [
            push(kept[s * count : (s + 1) * count].astype(jnp.bfloat16), axis, stride, size, s)
            for s in range(1, size)
        ]
        kept = kept[:count]
        for m in moved:
            kept = kept + m.astype(jnp.float32)
    return kept.astype(jnp.bfloat16)


def expert_body(me_ref, *refs, places, hidden_steps, experts, features):
    pieces = refs[: len(places)]
    gate_ref, up_ref, down_ref, keep_ref, send_ref, x_ref, h_ref, w_ref, sem = refs[len(places) :]
    step = pl.program_id(0)

    @pl.when(step == 0)
    def load_rows():
        copies = []
        for n, (piece, (row, lane)) in enumerate(zip(pieces, places, strict=True)):
            rows, lanes = piece.shape
            copies.append(
                pltpu.make_async_copy(
                    piece, x_ref.at[pl.ds(row, rows), pl.ds(lane, lanes)], sem.at[n]
                )
            )
        for copy in copies:
            copy.start()
        for copy in copies:
            copy.wait()
        tags = x_ref[:, features:].astype(jnp.float32)
        lane = lax.broadcasted_iota(jnp.int32, tags.shape, 1)
        mine = (lane % experts == me_ref[0]) & (lane < 3 * experts)
        w_ref[...] = jnp.sum(jnp.where(mine, tags, 0.0), axis=1, keepdims=True)

    block = gate_ref.shape[1]
    for n in range(hidden_steps):

        @pl.when(step == n)
        def first_layer(n=n):
            x = x_ref[:, :features]
            gate = jnp.dot(x, gate_ref[...], preferred_element_type=jnp.float32)
            up = jnp.dot(x, up_ref[...], preferred_element_type=jnp.float32)
            hidden = gate / (1.0 + jnp.exp(-gate)) * up
            h_ref[:, n * block : (n + 1) * block] = hidden.astype(jnp.bfloat16)

    @pl.when(step >= hidden_steps)
    def second_layer():
        part = jnp.dot(h_ref[...], down_ref[...], preferred_element_type=jnp.float32)
        total = part * w_ref[...]
        half = keep_ref.shape[0]
        keep_ref[...] = total[:half]
        send_ref[...] = total[half:].astype(jnp.bfloat16)


def expert_call(me, pieces, places, rows, experts, w_gate, w_up, w_down):
    features, hidden = w_gate.shape
    width = pieces[0].shape[1]
    block = 256
    wide = 512 if features % 512 == 0 else 128
    steps = hidden // block
    anywhere = pl.BlockSpec(memory_space=pl.ANY)
    outs = pl.BlockSpec((rows // 2, wide), lambda i: (0, jnp.maximum(i - steps, 0)))
    return pl.pallas_call(
        functools.partial(
            expert_body, places=places, hidden_steps=steps, experts=experts, features=features
        ),
        grid=(steps + features // wide,),
        in_specs=[
            pl.BlockSpec(memory_space=pltpu.SMEM),
            *[anywhere] * len(pieces),
            pl.BlockSpec((features, block), lambda i: (0, jnp.minimum(i, steps - 1))),
            pl.BlockSpec((features, block), lambda i: (0, jnp.minimum(i, steps - 1))),
            pl.BlockSpec((hidden, wide), lambda i: (0, jnp.maximum(i - steps, 0))),
        ],
        out_specs=[outs, outs],
        out_shape=[
            jax.ShapeDtypeStruct((rows // 2, features), jnp.float32),
            jax.ShapeDtypeStruct((rows // 2, features), jnp.bfloat16),
        ],
        scratch_shapes=[
            pltpu.VMEM((rows, width), jnp.bfloat16),
            pltpu.VMEM((rows, hidden), jnp.bfloat16),
            pltpu.VMEM((rows, 1), jnp.float32),
            pltpu.SemaphoreType.DMA((len(pieces),)),
        ],
        compiler_params=pltpu.CompilerParams(vmem_limit_bytes=58 << 20),
        name="expert",
    )(me, *pieces, w_gate, w_up, w_down)


def can_square(tokens, hidden):
    ep_size = lax.axis_size("ep")
    total = tokens * ep_size * lax.axis_size("dp")
    return lax.axis_size("dp") == 2 and ep_size % 4 == 0 and total <= 512 and hidden % 256 == 0


def experts_square(moe_input, expert_ids, gate_weights, w_gate, w_up, w_down):
    ep_size = lax.axis_size("ep")
    outer = ep_size // 4
    tokens, _ = moe_input.shape
    experts = jnp.arange(ep_size, dtype=jnp.int32)
    named = expert_ids[:, :, None] == experts[None, None, :]
    dense = jnp.sum(jnp.where(named, gate_weights[:, :, None], 0.0), axis=1)
    extra = split_exact(dense)
    lanes = -(-extra.shape[1] // 128) * 128
    extra = jnp.pad(extra, ((0, 0), (0, lanes - extra.shape[1])))
    rows = jnp.concatenate([moe_input, extra], axis=1)
    far = []
    for shift in range(1, outer):
        far.append(pull(rows, "ep", 4, outer, shift))
    own = jnp.concatenate([rows] + far, axis=0)
    by_x = pull(own, "dp", 1, 2, 1)
    by_y = pull(own, "ep", 2, 2, 1)
    both = pull(by_y, "dp", 1, 2, 1)
    near = [own, by_x, by_y, both]
    across = []
    for piece in near:
        across.append(pull(piece, "ep", 1, 2, 1))
    block = own.shape[0]
    places = [(n * block, 0) for n in range(8)]
    me = lax.axis_index("ep").astype(jnp.int32).reshape(1)
    keep, send = expert_call(
        me, near + across, tuple(places), 8 * block, ep_size, w_gate[0], w_up[0], w_down[0]
    )
    got = pull(send, "ep", 1, 2, 1)
    yield None
    keep = keep + got.astype(jnp.float32)
    own, by_x, by_y, both = (keep[n * block : (n + 1) * block] for n in range(4))
    got_both = pull(both.astype(jnp.bfloat16), "ep", 2, 2, 1)
    got_y = pull(by_y.astype(jnp.bfloat16), "ep", 2, 2, 1)
    yield None
    by_x = by_x + got_both.astype(jnp.float32)
    got_x = pull(by_x.astype(jnp.bfloat16), "dp", 1, 2, 1)
    yield None
    own = own + got_x.astype(jnp.float32) + got_y.astype(jnp.float32)
    got = []
    for shift in range(1, outer):
        piece = own[shift * tokens : (shift + 1) * tokens].astype(jnp.bfloat16)
        got.append(push(piece, "ep", 4, outer, shift))
    yield None
    total = own[:tokens]
    for piece in got:
        total = total + piece.astype(jnp.float32)
    yield total.astype(jnp.bfloat16)


def on_device(
    queries,
    suffix_latent,
    page_pool,
    page_owner,
    page_slot,
    prefix_len,
    moe_input,
    expert_ids,
    gate_weights,
    w_gate,
    w_up,
    w_down,
):
    packed, numbers = fetch_pages(page_pool, page_owner, page_slot)
    moe_args = (moe_input, expert_ids, gate_weights, w_gate, w_up, w_down)
    head_count = queries.shape[1] // KEY
    ranks = len(packed)

    def phase(rank, start, count, heads, before, so_far):
        return attend(
            queries,
            packed[rank],
            suffix_latent,
            numbers[rank],
            prefix_len,
            start,
            count,
            heads,
            before,
            rank == ranks - 1,
            so_far,
        )

    if ranks != 2 or not can_square(moe_input.shape[0], w_gate.shape[2]):
        moe_output = experts_staged(*moe_args)
        state = None
        for rank in range(ranks):
            state = phase(rank, 0, head_count, 2, state, None)
        return (state, moe_output)
    stages = experts_square(*moe_args)
    heads = 4
    half = head_count // (2 * heads) * heads
    parts = [(0, half), (half, head_count - half)]
    states = []
    for part in parts:
        next(stages)
        states.append(phase(0, *part, heads, None, None))
    attn_context = None
    for n, part in enumerate(parts):
        next(stages)
        attn_context = phase(1, *part, heads, states[n], attn_context)
    moe_output = next(stages)
    return (attn_context, moe_output)


def solution(mesh):
    return jax.shard_map(
        on_device,
        mesh=mesh,
        in_specs=(
            P("ep", "dp"),
            P("ep", None),
            P("ep", None),
            P("ep", None),
            P("ep", None),
            P("ep"),
            P(("dp", "ep"), None),
            P(("dp", "ep"), None),
            P(("dp", "ep"), None),
            P("ep", None, "dp"),
            P("ep", None, "dp"),
            P("ep", "dp", None),
        ),
        out_specs=(P("ep", "dp"), P(("dp", "ep"), None)),
        check_vma=False,
    )
```

```python
import functools
import math

import jax
import jax.numpy as jnp
from jax import lax
from jax.experimental import pallas as pl
from jax.experimental.pallas import tpu as pltpu
from jax.sharding import PartitionSpec as P


LATENT = 512
ROPE = 64
KEY = LATENT + ROPE
PAGE = 64
LANES = 128

score_scale = 0.07216878364870322
neg_large = -1e30


def partner(pos, shift, size):
    return pos ^ shift if size & (size - 1) == 0 else (pos + shift) % size


def pull(values, axis, stride, size, shift, back=False):
    total = lax.axis_size(axis)
    pairs = []
    for dst in range(total):
        pos = (dst // stride) % size
        src = dst + (partner(pos, shift, size) - pos) * stride
        pairs.append((dst, src) if back else (src, dst))
    return lax.ppermute(values, axis, pairs)


def push(values, axis, stride, size, shift):
    return pull(values, axis, stride, size, shift, back=True)


def gather_stages():
    ep_size = lax.axis_size("ep")
    inner = 2 if ep_size % 2 == 0 else 1
    middle = 2 if ep_size % (2 * inner) == 0 else 1
    outer = ep_size // (inner * middle)
    stages = [
        ("ep", inner * middle, outer),
        ("dp", 1, lax.axis_size("dp")),
        ("ep", inner, middle),
        ("ep", 1, inner),
    ]
    return [stage for stage in stages if stage[2] > 1]


def attention_body(*refs, heads, together, tail, begins, ends, aliased):
    number_ref, length_ref, q_ref, packed_ref, *refs = refs
    if tail:
        suffix_ref, *refs = refs
    if not begins:
        acc_in_ref, state_in_ref, *refs = refs
    refs = refs[aliased:]
    if ends:
        o_ref, *refs = refs
    else:
        acc_ref, state_ref, *refs = refs
    k_ref, rotary_ref, bias_ref, sem = refs
    tokens = q_ref.shape[0]
    steps = rotary_ref.shape[0]
    prefix = steps * PAGE
    slabs = LATENT // LANES
    factor = score_scale * math.log2(math.e)

    @pl.when(pl.program_id(0) == 0)
    def load_keys():
        copies = []
        for t in range(slabs):
            copies.append(
                pltpu.make_async_copy(
                    packed_ref.at[:, pl.ds(t * PAGE, PAGE)],
                    k_ref.at[pl.ds(0, steps), :, pl.ds(t * LANES, LANES)],
                    sem.at[t],
                )
            )
        last = packed_ref.at[:, pl.ds(slabs * PAGE, PAGE // 2)]
        copies.append(pltpu.make_async_copy(last, rotary_ref, sem.at[slabs]))
        if tail:
            for n in range(tail // PAGE):
                copies.append(
                    pltpu.make_async_copy(
                        suffix_ref.at[pl.ds(n * PAGE, PAGE)],
                        k_ref.at[steps + n],
                        sem.at[slabs + 1 + n],
                    )
                )
        for copy in copies:
            copy.start()
        lane = lax.broadcasted_iota(jnp.int32, (1, 2 * PAGE), 1)
        for pair in range(steps // 2):
            low = number_ref[2 * pair] * PAGE
            high = number_ref[2 * pair + 1] * PAGE - PAGE
            position = lane + jnp.where(lane < PAGE, low, high)
            seen = jnp.where(position < length_ref[0], 0.0, neg_large)
            bias_ref[:, 2 * PAGE * pair : 2 * PAGE * (pair + 1)] = seen.astype(jnp.float32)
        for copy in copies:
            copy.wait()
        half = PAGE // 2
        for n in range(steps):
            both = rotary_ref[n]
            k_ref[n, :half, LATENT:] = both[:, :ROPE]
            k_ref[n, half:, LATENT:] = both[:, ROPE:]

    bias = bias_ref[...]
    keys = k_ref[...].reshape(prefix + tail, KEY)
    if tail:
        row = lax.broadcasted_iota(jnp.int32, (tokens, tail), 0)
        col = lax.broadcasted_iota(jnp.int32, (tokens, tail), 1)
        causal = jnp.where(col <= row, 0.0, neg_large).astype(jnp.float32)
        causal = jnp.concatenate([causal] * together, axis=0)
    for first in range(0, heads, together):
        group = range(first, first + together)
        q = jnp.concatenate([q_ref[:, h * KEY : (h + 1) * KEY] for h in group], axis=0)
        s = lax.dot_general(
            q, keys, (((1,), (1,)), ((), ())), preferred_element_type=jnp.float32
        )
        blocks = [s[:, :prefix] + bias]
        if tail:
            blocks.append(s[:, prefix:] + causal)
        tops = [jnp.max(block, axis=1, keepdims=True) for block in blocks]
        if not begins:
            states = [state_in_ref[:, h * LANES : (h + 1) * LANES] for h in group]
            state = jnp.concatenate(states, axis=0)
            before = state[:, :1]
            tops.append(before)
        m = functools.reduce(jnp.maximum, tops)
        shift = m * factor
        powers = [jnp.exp2(block * factor - shift) for block in blocks]
        total = sum(jnp.sum(power, axis=1, keepdims=True) for power in powers)
        p = jnp.concatenate([power.astype(jnp.bfloat16) for power in powers], axis=1)
        acc = jnp.dot(p, keys[:, :LATENT], preferred_element_type=jnp.float32)
        if not begins:
            scale = jnp.exp2(before * factor - shift)
            total = total + state[:, LANES - 1 :] * scale
            olds = [acc_in_ref[:, h * LATENT : (h + 1) * LATENT] for h in group]
            acc = acc + jnp.concatenate(olds, axis=0) * scale
        if ends:
            acc = acc / total
        else:
            lane = lax.broadcasted_iota(jnp.int32, (acc.shape[0], LANES), 1)
            state = jnp.where(lane < LANES // 2, m, total)
        for n, h in enumerate(group):
            rows = slice(n * tokens, (n + 1) * tokens)
            if ends:
                o_ref[:, h * LATENT : (h + 1) * LATENT] = acc[rows].astype(jnp.bfloat16)
            else:
                acc_ref[:, h * LATENT : (h + 1) * LATENT] = acc[rows]
                state_ref[:, h * LANES : (h + 1) * LANES] = state[rows]


def attend(
    queries, packed, suffix, numbers, length, start, count, heads, before=None, ends=True, so_far=None
):
    tokens = queries.shape[0]
    head_count = queries.shape[1] // KEY
    steps = packed.shape[0]
    prefix = steps * PAGE
    begins = before is None
    tail = suffix.shape[0] if begins else 0
    together = 4 if heads % 4 == 0 and prefix <= 2048 else 2
    offset = start // heads
    aliased = 0 if so_far is None else 1
    scalars = pl.BlockSpec(memory_space=pltpu.SMEM)
    anywhere = pl.BlockSpec(memory_space=pl.ANY)
    operands = [numbers, length, queries, packed]
    in_specs = [
        scalars,
        scalars,
        pl.BlockSpec((tokens, heads * KEY), lambda i: (0, i + offset)),
        anywhere,
    ]
    if begins:
        operands.append(suffix)
        in_specs.append(anywhere)
    else:
        operands += before
        in_specs += [
            pl.BlockSpec((tokens, heads * LATENT), lambda i: (0, i)),
            pl.BlockSpec((tokens, heads * LANES), lambda i: (0, i)),
        ]
    if aliased:
        operands.append(so_far)
        in_specs.append(anywhere)
    if ends:
        out_specs = pl.BlockSpec((tokens, heads * LATENT), lambda i: (0, i + offset))
        out_shape = jax.ShapeDtypeStruct((tokens, head_count * LATENT), jnp.bfloat16)
    else:
        out_specs = [
            pl.BlockSpec((tokens, heads * LATENT), lambda i: (0, i)),
            pl.BlockSpec((tokens, heads * LANES), lambda i: (0, i)),
        ]
        out_shape = [
            jax.ShapeDtypeStruct((tokens, count * LATENT), jnp.float32),
            jax.ShapeDtypeStruct((tokens, count * LANES), jnp.float32),
        ]
    return pl.pallas_call(
        functools.partial(
            attention_body,
            heads=heads,
            together=together,
            tail=tail,
            begins=begins,
            ends=ends,
            aliased=aliased,
        ),
        grid=(count // heads,),
        in_specs=in_specs,
        out_specs=out_specs,
        out_shape=out_shape,
        scratch_shapes=[
            pltpu.VMEM((steps + tail // PAGE, PAGE, KEY), jnp.bfloat16),
            pltpu.VMEM((steps, PAGE // 2, LANES), jnp.bfloat16),
            pltpu.VMEM((1, prefix), jnp.float32),
            pltpu.SemaphoreType.DMA((LATENT // LANES + 1 + tail // PAGE,)),
        ],
        input_output_aliases={len(operands) - 1: 0} if aliased else {},
        compiler_params=pltpu.CompilerParams(vmem_limit_bytes=58 << 20),
        name="attend",
    )(*operands)


def fetch_pages(page_pool, page_owner, page_slot):
    ep_size = lax.axis_size("ep")
    pages = page_owner.shape[1]
    ranks = (pages + ep_size - 1) // ep_size
    page_id = jnp.arange(pages, dtype=jnp.int32)
    owners = jnp.arange(ep_size, dtype=jnp.int32)
    rank_id = jnp.arange(ranks, dtype=jnp.int32)
    match = (page_owner[0][None, None, :] == owners[:, None, None]) & (
        page_id[None, None, :] // ep_size == rank_id[None, :, None]
    )
    wanted = jnp.sum(jnp.where(match, page_slot[0][None, None, :], 0), axis=2)
    asked = lax.all_to_all(wanted, "ep", split_axis=0, concat_axis=0, tiled=True)
    pool = page_pool.reshape(page_pool.shape[0], PAGE, KEY)
    place = jnp.arange(ep_size, dtype=jnp.int32)

    def number(first):
        low = first * ep_size
        ids = low + jnp.arange(min(ep_size, pages), dtype=jnp.int32)
        held = lax.dynamic_slice_in_dim(page_owner[0], low, min(ep_size, pages))
        hit = place[:, None] == held[None, :]
        return pages + jnp.sum(jnp.where(hit, ids[None, :] - pages, 0), axis=1)

    dp_size = lax.axis_size("dp")
    if ranks == dp_size and pages == ranks * ep_size:
        plane = lax.axis_index("dp").astype(jnp.int32)
        chosen = pick_pages(plane.reshape(1), asked, pool)
        own = lax.all_to_all(chosen, "ep", split_axis=0, concat_axis=0, tiled=True)
        fetched, numbers = [own], [number(plane)]
        for shift in range(1, dp_size):
            fetched.append(pull(own, "dp", 1, dp_size, shift))
            numbers.append(number(partner(plane, jnp.int32(shift), dp_size)))
        return fetched, numbers
    fetched, numbers = [], []
    for r in range(ranks):
        chosen = pick_pages(jnp.full((1,), r, jnp.int32), asked, pool)
        fetched.append(lax.all_to_all(chosen, "ep", split_axis=0, concat_axis=0, tiled=True))
        numbers.append(number(jnp.int32(r)))
    return fetched, numbers


def pick_body(rank_ref, asked_ref, pool_ref, out_ref):
    slabs = LATENT // LANES
    half = PAGE // 2
    for n in range(asked_ref.shape[0]):
        page = pool_ref[asked_ref[n, rank_ref[0]]]
        for t in range(slabs):
            out_ref[n, t * PAGE : (t + 1) * PAGE] = page[:, t * LANES : (t + 1) * LANES]
        rotary = page[:, LATENT:]
        out_ref[n, slabs * PAGE :] = jnp.concatenate([rotary[:half], rotary[half:]], axis=1)


def pick_pages(rank, asked, pool):
    scalars = pl.BlockSpec(memory_space=pltpu.SMEM)
    whole = pl.BlockSpec(memory_space=pltpu.VMEM)
    shape = (asked.shape[0], PAGE * KEY // LANES, LANES)
    return pl.pallas_call(
        pick_body,
        in_specs=[scalars, scalars, whole],
        out_specs=whole,
        out_shape=jax.ShapeDtypeStruct(shape, pool.dtype),
        name="pick",
    )(rank, asked, pool)


def split_exact(values):
    high = values.astype(jnp.bfloat16)
    rest = values - high.astype(jnp.float32)
    mid = rest.astype(jnp.bfloat16)
    low = (rest - mid.astype(jnp.float32)).astype(jnp.bfloat16)
    return jnp.concatenate([high, mid, low], axis=1)


def experts_staged(moe_input, expert_ids, gate_weights, w_gate, w_up, w_down):
    ep_size = lax.axis_size("ep")
    _, features = moe_input.shape
    experts = jnp.arange(ep_size, dtype=jnp.int32)
    named = expert_ids[:, :, None] == experts[None, None, :]
    dense = jnp.sum(jnp.where(named, gate_weights[:, :, None], 0.0), axis=1)
    extra = split_exact(dense)
    lanes = -(-extra.shape[1] // 128) * 128
    extra = jnp.pad(extra, ((0, 0), (0, lanes - extra.shape[1])))
    rows = jnp.concatenate([moe_input, extra], axis=1)
    stages = gather_stages()
    for axis, stride, size in stages:
        rows = jnp.concatenate(
            [rows] + [pull(rows, axis, stride, size, shift) for shift in range(1, size)], axis=0
        )
    inputs = rows[:, :features]
    parts = rows[:, features : features + 3 * ep_size].astype(jnp.float32)
    parts = parts.reshape(-1, 3, ep_size)
    here = (experts == lax.axis_index("ep"))[None, None, :]
    parts = jnp.sum(jnp.where(here, parts, 0.0), axis=2)
    weight = (parts[:, 0] + parts[:, 1] + parts[:, 2])[:, None]
    gate_proj = jnp.dot(inputs, w_gate[0], preferred_element_type=jnp.float32)
    up_proj = jnp.dot(inputs, w_up[0], preferred_element_type=jnp.float32)
    hidden = (jax.nn.silu(gate_proj) * up_proj).astype(jnp.bfloat16)
    kept = jnp.dot(hidden, w_down[0], preferred_element_type=jnp.float32) * weight
    for axis, stride, size in reversed(stages):
        count = kept.shape[0] // size
        moved = [
            push(kept[s * count : (s + 1) * count].astype(jnp.bfloat16), axis, stride, size, s)
            for s in range(1, size)
        ]
        kept = kept[:count]
        for m in moved:
            kept = kept + m.astype(jnp.float32)
    return kept.astype(jnp.bfloat16)


def expert_body(me_ref, *refs, places, hidden_steps, experts, features):
    pieces = refs[: len(places)]
    gate_ref, up_ref, down_ref, keep_ref, send_ref, x_ref, h_ref, w_ref, sem = refs[len(places) :]
    step = pl.program_id(0)

    @pl.when(step == 0)
    def load_rows():
        copies = []
        for n, (piece, (row, lane)) in enumerate(zip(pieces, places, strict=True)):
            rows, lanes = piece.shape
            copies.append(
                pltpu.make_async_copy(
                    piece, x_ref.at[pl.ds(row, rows), pl.ds(lane, lanes)], sem.at[n]
                )
            )
        for copy in copies:
            copy.start()
        for copy in copies:
            copy.wait()
        tags = x_ref[:, features:].astype(jnp.float32)
        lane = lax.broadcasted_iota(jnp.int32, tags.shape, 1)
        mine = (lane % experts == me_ref[0]) & (lane < 3 * experts)
        w_ref[...] = jnp.sum(jnp.where(mine, tags, 0.0), axis=1, keepdims=True)

    block = gate_ref.shape[1]
    for n in range(hidden_steps):

        @pl.when(step == n)
        def first_layer(n=n):
            x = x_ref[:, :features]
            gate = jnp.dot(x, gate_ref[...], preferred_element_type=jnp.float32)
            up = jnp.dot(x, up_ref[...], preferred_element_type=jnp.float32)
            hidden = gate / (1.0 + jnp.exp(-gate)) * up
            h_ref[:, n * block : (n + 1) * block] = hidden.astype(jnp.bfloat16)

    @pl.when(step >= hidden_steps)
    def second_layer():
        part = jnp.dot(h_ref[...], down_ref[...], preferred_element_type=jnp.float32)
        total = part * w_ref[...]
        half = keep_ref.shape[0]
        keep_ref[...] = total[:half]
        send_ref[...] = total[half:].astype(jnp.bfloat16)


def expert_call(me, pieces, places, rows, experts, w_gate, w_up, w_down):
    features, hidden = w_gate.shape
    width = pieces[0].shape[1]
    block = 256
    wide = 512 if features % 512 == 0 else 128
    steps = hidden // block
    anywhere = pl.BlockSpec(memory_space=pl.ANY)
    outs = pl.BlockSpec((rows // 2, wide), lambda i: (0, jnp.maximum(i - steps, 0)))
    return pl.pallas_call(
        functools.partial(
            expert_body, places=places, hidden_steps=steps, experts=experts, features=features
        ),
        grid=(steps + features // wide,),
        in_specs=[
            pl.BlockSpec(memory_space=pltpu.SMEM),
            *[anywhere] * len(pieces),
            pl.BlockSpec((features, block), lambda i: (0, jnp.minimum(i, steps - 1))),
            pl.BlockSpec((features, block), lambda i: (0, jnp.minimum(i, steps - 1))),
            pl.BlockSpec((hidden, wide), lambda i: (0, jnp.maximum(i - steps, 0))),
        ],
        out_specs=[outs, outs],
        out_shape=[
            jax.ShapeDtypeStruct((rows // 2, features), jnp.float32),
            jax.ShapeDtypeStruct((rows // 2, features), jnp.bfloat16),
        ],
        scratch_shapes=[
            pltpu.VMEM((rows, width), jnp.bfloat16),
            pltpu.VMEM((rows, hidden), jnp.bfloat16),
            pltpu.VMEM((rows, 1), jnp.float32),
            pltpu.SemaphoreType.DMA((len(pieces),)),
        ],
        compiler_params=pltpu.CompilerParams(vmem_limit_bytes=58 << 20),
        name="expert",
    )(me, *pieces, w_gate, w_up, w_down)


def can_square(tokens, hidden):
    ep_size = lax.axis_size("ep")
    total = tokens * ep_size * lax.axis_size("dp")
    return lax.axis_size("dp") == 2 and ep_size % 4 == 0 and total <= 512 and hidden % 256 == 0


def experts_square(moe_input, expert_ids, gate_weights, w_gate, w_up, w_down):
    ep_size = lax.axis_size("ep")
    outer = ep_size // 4
    tokens, _ = moe_input.shape
    experts = jnp.arange(ep_size, dtype=jnp.int32)
    named = expert_ids[:, :, None] == experts[None, None, :]
    dense = jnp.sum(jnp.where(named, gate_weights[:, :, None], 0.0), axis=1)
    extra = split_exact(dense)
    lanes = -(-extra.shape[1] // 128) * 128
    extra = jnp.pad(extra, ((0, 0), (0, lanes - extra.shape[1])))
    rows = jnp.concatenate([moe_input, extra], axis=1)
    far = []
    for shift in range(1, outer):
        far.append(pull(rows, "ep", 4, outer, shift))
    own = jnp.concatenate([rows] + far, axis=0)
    by_x = pull(own, "dp", 1, 2, 1)
    by_y = pull(own, "ep", 2, 2, 1)
    both = pull(by_y, "dp", 1, 2, 1)
    near = [own, by_x, by_y, both]
    across = []
    for piece in near:
        across.append(pull(piece, "ep", 1, 2, 1))
    block = own.shape[0]
    places = [(n * block, 0) for n in range(8)]
    me = lax.axis_index("ep").astype(jnp.int32).reshape(1)
    keep, send = expert_call(
        me, near + across, tuple(places), 8 * block, ep_size, w_gate[0], w_up[0], w_down[0]
    )
    got = pull(send, "ep", 1, 2, 1)
    yield None
    keep = keep + got.astype(jnp.float32)
    own, by_x, by_y, both = (keep[n * block : (n + 1) * block] for n in range(4))
    got_both = pull(both.astype(jnp.bfloat16), "ep", 2, 2, 1)
    got_y = pull(by_y.astype(jnp.bfloat16), "ep", 2, 2, 1)
    yield None
    by_x = by_x + got_both.astype(jnp.float32)
    got_x = pull(by_x.astype(jnp.bfloat16), "dp", 1, 2, 1)
    yield None
    own = own + got_x.astype(jnp.float32) + got_y.astype(jnp.float32)
    got = []
    for shift in range(1, outer):
        piece = own[shift * tokens : (shift + 1) * tokens].astype(jnp.bfloat16)
        got.append(push(piece, "ep", 4, outer, shift))
    yield None
    total = own[:tokens]
    for piece in got:
        total = total + piece.astype(jnp.float32)
    yield total.astype(jnp.bfloat16)


def on_device(
    queries,
    suffix_latent,
    page_pool,
    page_owner,
    page_slot,
    prefix_len,
    moe_input,
    expert_ids,
    gate_weights,
    w_gate,
    w_up,
    w_down,
):
    packed, numbers = fetch_pages(page_pool, page_owner, page_slot)
    moe_args = (moe_input, expert_ids, gate_weights, w_gate, w_up, w_down)
    head_count = queries.shape[1] // KEY
    ranks = len(packed)

    def phase(rank, start, count, heads, before, so_far):
        return attend(
            queries,
            packed[rank],
            suffix_latent,
            numbers[rank],
            prefix_len,
            start,
            count,
            heads,
            before,
            rank == ranks - 1,
            so_far,
        )

    if ranks != 2 or not can_square(moe_input.shape[0], w_gate.shape[2]):
        moe_output = experts_staged(*moe_args)
        state = None
        for rank in range(ranks):
            state = phase(rank, 0, head_count, 2, state, None)
        return (state, moe_output)
    stages = experts_square(*moe_args)
    heads = 4
    half = head_count // (2 * heads) * heads
    parts = [(0, half), (half, head_count - half)]
    states = []
    for part in parts:
        next(stages)
        states.append(phase(0, *part, heads, None, None))
    attn_context = None
    for n, part in enumerate(parts):
        next(stages)
        attn_context = phase(1, *part, heads, states[n], attn_context)
    moe_output = next(stages)
    return (attn_context, moe_output)


def solution(mesh):
    return jax.shard_map(
        on_device,
        mesh=mesh,
        in_specs=(
            P("ep", "dp"),
            P("ep", None),
            P("ep", None),
            P("ep", None),
            P("ep", None),
            P("ep"),
            P(("dp", "ep"), None),
            P(("dp", "ep"), None),
            P(("dp", "ep"), None),
            P("ep", None, "dp"),
            P("ep", None, "dp"),
            P("ep", "dp", None),
        ),
        out_specs=(P("ep", "dp"), P(("dp", "ep"), None)),
        check_vma=False,
    )
```

```python
import functools
import math

import jax
import jax.numpy as jnp
from jax import lax
from jax.experimental import pallas as pl
from jax.experimental.pallas import tpu as pltpu
from jax.sharding import PartitionSpec as P


LATENT = 512
ROPE = 64
KEY = LATENT + ROPE
PAGE = 64
LANES = 128

score_scale = 0.07216878364870322
neg_large = -1e30


def partner(pos, shift, size):
    return pos ^ shift if size & (size - 1) == 0 else (pos + shift) % size


def pull(values, axis, stride, size, shift, back=False):
    total = lax.axis_size(axis)
    pairs = []
    for dst in range(total):
        pos = (dst // stride) % size
        src = dst + (partner(pos, shift, size) - pos) * stride
        pairs.append((dst, src) if back else (src, dst))
    return lax.ppermute(values, axis, pairs)


def push(values, axis, stride, size, shift):
    return pull(values, axis, stride, size, shift, back=True)


def gather_stages():
    ep_size = lax.axis_size("ep")
    inner = 2 if ep_size % 2 == 0 else 1
    middle = 2 if ep_size % (2 * inner) == 0 else 1
    outer = ep_size // (inner * middle)
    stages = [
        ("ep", inner * middle, outer),
        ("dp", 1, lax.axis_size("dp")),
        ("ep", inner, middle),
        ("ep", 1, inner),
    ]
    return [stage for stage in stages if stage[2] > 1]


def attention_body(*refs, heads, together, tail, begins, ends, aliased):
    number_ref, length_ref, q_ref, packed_ref, *refs = refs
    if tail:
        suffix_ref, *refs = refs
    if not begins:
        acc_in_ref, state_in_ref, *refs = refs
    refs = refs[aliased:]
    if ends:
        o_ref, *refs = refs
    else:
        acc_ref, state_ref, *refs = refs
    k_ref, rotary_ref, bias_ref, sem = refs
    tokens = q_ref.shape[0]
    steps = rotary_ref.shape[0]
    prefix = steps * PAGE
    slabs = LATENT // LANES
    factor = score_scale * math.log2(math.e)

    @pl.when(pl.program_id(0) == 0)
    def load_keys():
        copies = []
        for t in range(slabs):
            copies.append(
                pltpu.make_async_copy(
                    packed_ref.at[:, pl.ds(t * PAGE, PAGE)],
                    k_ref.at[pl.ds(0, steps), :, pl.ds(t * LANES, LANES)],
                    sem.at[t],
                )
            )
        last = packed_ref.at[:, pl.ds(slabs * PAGE, PAGE // 2)]
        copies.append(pltpu.make_async_copy(last, rotary_ref, sem.at[slabs]))
        if tail:
            for n in range(tail // PAGE):
                copies.append(
                    pltpu.make_async_copy(
                        suffix_ref.at[pl.ds(n * PAGE, PAGE)],
                        k_ref.at[steps + n],
                        sem.at[slabs + 1 + n],
                    )
                )
        for copy in copies:
            copy.start()
        lane = lax.broadcasted_iota(jnp.int32, (1, 2 * PAGE), 1)
        for pair in range(steps // 2):
            low = number_ref[2 * pair] * PAGE
            high = number_ref[2 * pair + 1] * PAGE - PAGE
            position = lane + jnp.where(lane < PAGE, low, high)
            seen = jnp.where(position < length_ref[0], 0.0, neg_large)
            bias_ref[:, 2 * PAGE * pair : 2 * PAGE * (pair + 1)] = seen.astype(jnp.float32)
        for copy in copies:
            copy.wait()
        half = PAGE // 2
        for n in range(steps):
            both = rotary_ref[n]
            k_ref[n, :half, LATENT:] = both[:, :ROPE]
            k_ref[n, half:, LATENT:] = both[:, ROPE:]

    bias = bias_ref[...]
    keys = k_ref[...].reshape(prefix + tail, KEY)
    if tail:
        row = lax.broadcasted_iota(jnp.int32, (tokens, tail), 0)
        col = lax.broadcasted_iota(jnp.int32, (tokens, tail), 1)
        causal = jnp.where(col <= row, 0.0, neg_large).astype(jnp.float32)
        causal = jnp.concatenate([causal] * together, axis=0)
    for first in range(0, heads, together):
        group = range(first, first + together)
        q = jnp.concatenate([q_ref[:, h * KEY : (h + 1) * KEY] for h in group], axis=0)
        s = lax.dot_general(
            q, keys, (((1,), (1,)), ((), ())), preferred_element_type=jnp.float32
        )
        blocks = [s[:, :prefix] + bias]
        if tail:
            blocks.append(s[:, prefix:] + causal)
        tops = [jnp.max(block, axis=1, keepdims=True) for block in blocks]
        if not begins:
            states = [state_in_ref[:, h * LANES : (h + 1) * LANES] for h in group]
            state = jnp.concatenate(states, axis=0)
            before = state[:, :1]
            tops.append(before)
        m = functools.reduce(jnp.maximum, tops)
        shift = m * factor
        powers = [jnp.exp2(block * factor - shift) for block in blocks]
        total = sum(jnp.sum(power, axis=1, keepdims=True) for power in powers)
        p = jnp.concatenate([power.astype(jnp.bfloat16) for power in powers], axis=1)
        acc = jnp.dot(p, keys[:, :LATENT], preferred_element_type=jnp.float32)
        if not begins:
            scale = jnp.exp2(before * factor - shift)
            total = total + state[:, LANES - 1 :] * scale
            olds = [acc_in_ref[:, h * LATENT : (h + 1) * LATENT] for h in group]
            acc = acc + jnp.concatenate(olds, axis=0) * scale
        if ends:
            acc = acc / total
        else:
            lane = lax.broadcasted_iota(jnp.int32, (acc.shape[0], LANES), 1)
            state = jnp.where(lane < LANES // 2, m, total)
        for n, h in enumerate(group):
            rows = slice(n * tokens, (n + 1) * tokens)
            if ends:
                o_ref[:, h * LATENT : (h + 1) * LATENT] = acc[rows].astype(jnp.bfloat16)
            else:
                acc_ref[:, h * LATENT : (h + 1) * LATENT] = acc[rows]
                state_ref[:, h * LANES : (h + 1) * LANES] = state[rows]


def attend(
    queries, packed, suffix, numbers, length, start, count, heads, before=None, ends=True, so_far=None
):
    tokens = queries.shape[0]
    head_count = queries.shape[1] // KEY
    steps = packed.shape[0]
    prefix = steps * PAGE
    begins = before is None
    tail = suffix.shape[0] if begins else 0
    together = 4 if heads % 4 == 0 and prefix <= 2048 else 2
    offset = start // heads
    aliased = 0 if so_far is None else 1
    scalars = pl.BlockSpec(memory_space=pltpu.SMEM)
    anywhere = pl.BlockSpec(memory_space=pl.ANY)
    operands = [numbers, length, queries, packed]
    in_specs = [
        scalars,
        scalars,
        pl.BlockSpec((tokens, heads * KEY), lambda i: (0, i + offset)),
        anywhere,
    ]
    if begins:
        operands.append(suffix)
        in_specs.append(anywhere)
    else:
        operands += before
        in_specs += [
            pl.BlockSpec((tokens, heads * LATENT), lambda i: (0, i + offset)),
            pl.BlockSpec((tokens, heads * LANES), lambda i: (0, i + offset)),
        ]
    if aliased:
        operands.append(so_far)
        in_specs.append(anywhere)
    if ends:
        out_specs = pl.BlockSpec((tokens, heads * LATENT), lambda i: (0, i + offset))
        out_shape = jax.ShapeDtypeStruct((tokens, head_count * LATENT), jnp.bfloat16)
    else:
        out_specs = [
            pl.BlockSpec((tokens, heads * LATENT), lambda i: (0, i)),
            pl.BlockSpec((tokens, heads * LANES), lambda i: (0, i)),
        ]
        out_shape = [
            jax.ShapeDtypeStruct((tokens, count * LATENT), jnp.float32),
            jax.ShapeDtypeStruct((tokens, count * LANES), jnp.float32),
        ]
    return pl.pallas_call(
        functools.partial(
            attention_body,
            heads=heads,
            together=together,
            tail=tail,
            begins=begins,
            ends=ends,
            aliased=aliased,
        ),
        grid=(count // heads,),
        in_specs=in_specs,
        out_specs=out_specs,
        out_shape=out_shape,
        scratch_shapes=[
            pltpu.VMEM((steps + tail // PAGE, PAGE, KEY), jnp.bfloat16),
            pltpu.VMEM((steps, PAGE // 2, LANES), jnp.bfloat16),
            pltpu.VMEM((1, prefix), jnp.float32),
            pltpu.SemaphoreType.DMA((LATENT // LANES + 1 + tail // PAGE,)),
        ],
        input_output_aliases={len(operands) - 1: 0} if aliased else {},
        compiler_params=pltpu.CompilerParams(vmem_limit_bytes=58 << 20),
        name="attend",
    )(*operands)


def lay_body(first_ref, second_ref, rows_ref, out_ref):
    out_ref[...] = rows_ref[...]


def lay_rows(first, second, rows):
    scalars = pl.BlockSpec(memory_space=pltpu.SMEM)
    whole = pl.BlockSpec(memory_space=pltpu.VMEM)
    return pl.pallas_call(
        lay_body,
        in_specs=[scalars, scalars, whole],
        out_specs=whole,
        out_shape=jax.ShapeDtypeStruct(rows.shape, rows.dtype),
        name="lay",
    )(first, second, rows)


def fetch_pages(page_pool, page_owner, page_slot):
    ep_size = lax.axis_size("ep")
    pages = page_owner.shape[1]
    ranks = (pages + ep_size - 1) // ep_size
    page_id = jnp.arange(pages, dtype=jnp.int32)
    owners = jnp.arange(ep_size, dtype=jnp.int32)
    rank_id = jnp.arange(ranks, dtype=jnp.int32)
    match = (page_owner[0][None, None, :] == owners[:, None, None]) & (
        page_id[None, None, :] // ep_size == rank_id[None, :, None]
    )
    wanted = jnp.sum(jnp.where(match, page_slot[0][None, None, :], 0), axis=2)
    asked = lax.all_to_all(wanted, "ep", split_axis=0, concat_axis=0, tiled=True)
    pool = page_pool.reshape(page_pool.shape[0], PAGE, KEY)
    place = jnp.arange(ep_size, dtype=jnp.int32)

    def number(first):
        low = first * ep_size
        ids = low + jnp.arange(min(ep_size, pages), dtype=jnp.int32)
        held = lax.dynamic_slice_in_dim(page_owner[0], low, min(ep_size, pages))
        hit = place[:, None] == held[None, :]
        return pages + jnp.sum(jnp.where(hit, ids[None, :] - pages, 0), axis=1)

    dp_size = lax.axis_size("dp")
    if ranks == dp_size and pages == ranks * ep_size:
        plane = lax.axis_index("dp").astype(jnp.int32)
        chosen = pick_pages(plane.reshape(1), asked, pool)
        own = lax.all_to_all(chosen, "ep", split_axis=0, concat_axis=0, tiled=True)
        fetched, numbers = [own], [number(plane)]
        for shift in range(1, dp_size):
            fetched.append(pull(own, "dp", 1, dp_size, shift))
            numbers.append(number(partner(plane, jnp.int32(shift), dp_size)))
        return fetched, numbers
    fetched, numbers = [], []
    for r in range(ranks):
        chosen = pick_pages(jnp.full((1,), r, jnp.int32), asked, pool)
        fetched.append(lax.all_to_all(chosen, "ep", split_axis=0, concat_axis=0, tiled=True))
        numbers.append(number(jnp.int32(r)))
    return fetched, numbers


def pick_body(rank_ref, asked_ref, pool_ref, out_ref):
    slabs = LATENT // LANES
    half = PAGE // 2
    for n in range(asked_ref.shape[0]):
        page = pool_ref[asked_ref[n, rank_ref[0]]]
        for t in range(slabs):
            out_ref[n, t * PAGE : (t + 1) * PAGE] = page[:, t * LANES : (t + 1) * LANES]
        rotary = page[:, LATENT:]
        out_ref[n, slabs * PAGE :] = jnp.concatenate([rotary[:half], rotary[half:]], axis=1)


def pick_pages(rank, asked, pool):
    scalars = pl.BlockSpec(memory_space=pltpu.SMEM)
    whole = pl.BlockSpec(memory_space=pltpu.VMEM)
    shape = (asked.shape[0], PAGE * KEY // LANES, LANES)
    return pl.pallas_call(
        pick_body,
        in_specs=[scalars, scalars, whole],
        out_specs=whole,
        out_shape=jax.ShapeDtypeStruct(shape, pool.dtype),
        name="pick",
    )(rank, asked, pool)


def split_exact(values):
    high = values.astype(jnp.bfloat16)
    rest = values - high.astype(jnp.float32)
    mid = rest.astype(jnp.bfloat16)
    low = (rest - mid.astype(jnp.float32)).astype(jnp.bfloat16)
    return jnp.concatenate([high, mid, low], axis=1)


def experts_staged(moe_input, expert_ids, gate_weights, w_gate, w_up, w_down):
    ep_size = lax.axis_size("ep")
    _, features = moe_input.shape
    experts = jnp.arange(ep_size, dtype=jnp.int32)
    named = expert_ids[:, :, None] == experts[None, None, :]
    dense = jnp.sum(jnp.where(named, gate_weights[:, :, None], 0.0), axis=1)
    extra = split_exact(dense)
    lanes = -(-extra.shape[1] // 128) * 128
    extra = jnp.pad(extra, ((0, 0), (0, lanes - extra.shape[1])))
    rows = jnp.concatenate([moe_input, extra], axis=1)
    stages = gather_stages()
    for axis, stride, size in stages:
        rows = jnp.concatenate(
            [rows] + [pull(rows, axis, stride, size, shift) for shift in range(1, size)], axis=0
        )
    inputs = rows[:, :features]
    parts = rows[:, features : features + 3 * ep_size].astype(jnp.float32)
    parts = parts.reshape(-1, 3, ep_size)
    here = (experts == lax.axis_index("ep"))[None, None, :]
    parts = jnp.sum(jnp.where(here, parts, 0.0), axis=2)
    weight = (parts[:, 0] + parts[:, 1] + parts[:, 2])[:, None]
    gate_proj = jnp.dot(inputs, w_gate[0], preferred_element_type=jnp.float32)
    up_proj = jnp.dot(inputs, w_up[0], preferred_element_type=jnp.float32)
    hidden = (jax.nn.silu(gate_proj) * up_proj).astype(jnp.bfloat16)
    kept = jnp.dot(hidden, w_down[0], preferred_element_type=jnp.float32) * weight
    for axis, stride, size in reversed(stages):
        count = kept.shape[0] // size
        moved = [
            push(kept[s * count : (s + 1) * count].astype(jnp.bfloat16), axis, stride, size, s)
            for s in range(1, size)
        ]
        kept = kept[:count]
        for m in moved:
            kept = kept + m.astype(jnp.float32)
    return kept.astype(jnp.bfloat16)


def expert_body(me_ref, *refs, places, hidden_steps, experts, features):
    pieces = refs[: len(places)]
    gate_ref, up_ref, down_ref, keep_ref, send_ref, x_ref, h_ref, w_ref, sem = refs[len(places) :]
    step = pl.program_id(0)

    @pl.when(step == 0)
    def load_rows():
        copies = []
        for n, (piece, (row, lane)) in enumerate(zip(pieces, places, strict=True)):
            rows, lanes = piece.shape
            copies.append(
                pltpu.make_async_copy(
                    piece, x_ref.at[pl.ds(row, rows), pl.ds(lane, lanes)], sem.at[n]
                )
            )
        for copy in copies:
            copy.start()
        for copy in copies:
            copy.wait()
        tags = x_ref[:, features:].astype(jnp.float32)
        lane = lax.broadcasted_iota(jnp.int32, tags.shape, 1)
        mine = (lane % experts == me_ref[0]) & (lane < 3 * experts)
        w_ref[...] = jnp.sum(jnp.where(mine, tags, 0.0), axis=1, keepdims=True)

    block = gate_ref.shape[1]
    for n in range(hidden_steps):

        @pl.when(step == n)
        def first_layer(n=n):
            x = x_ref[:, :features]
            gate = jnp.dot(x, gate_ref[...], preferred_element_type=jnp.float32)
            up = jnp.dot(x, up_ref[...], preferred_element_type=jnp.float32)
            hidden = gate / (1.0 + jnp.exp(-gate)) * up
            h_ref[:, n * block : (n + 1) * block] = hidden.astype(jnp.bfloat16)

    @pl.when(step >= hidden_steps)
    def second_layer():
        part = jnp.dot(h_ref[...], down_ref[...], preferred_element_type=jnp.float32)
        total = part * w_ref[...]
        half = keep_ref.shape[0]
        keep_ref[...] = total[:half]
        send_ref[...] = total[half:].astype(jnp.bfloat16)


def expert_call(me, pieces, places, rows, experts, w_gate, w_up, w_down):
    features, hidden = w_gate.shape
    width = pieces[0].shape[1]
    block = 256
    wide = features // 2 if features % 512 == 0 else 128
    steps = hidden // block
    anywhere = pl.BlockSpec(memory_space=pl.ANY)
    outs = pl.BlockSpec((rows // 2, wide), lambda i: (0, jnp.maximum(i - steps, 0)))
    return pl.pallas_call(
        functools.partial(
            expert_body, places=places, hidden_steps=steps, experts=experts, features=features
        ),
        grid=(steps + features // wide,),
        in_specs=[
            pl.BlockSpec(memory_space=pltpu.SMEM),
            *[anywhere] * len(pieces),
            pl.BlockSpec((features, block), lambda i: (0, jnp.minimum(i, steps - 1))),
            pl.BlockSpec((features, block), lambda i: (0, jnp.minimum(i, steps - 1))),
            pl.BlockSpec((hidden, wide), lambda i: (0, jnp.maximum(i - steps, 0))),
        ],
        out_specs=[outs, outs],
        out_shape=[
            jax.ShapeDtypeStruct((rows // 2, features), jnp.float32),
            jax.ShapeDtypeStruct((rows // 2, features), jnp.bfloat16),
        ],
        scratch_shapes=[
            pltpu.VMEM((rows, width), jnp.bfloat16),
            pltpu.VMEM((rows, hidden), jnp.bfloat16),
            pltpu.VMEM((rows, 1), jnp.float32),
            pltpu.SemaphoreType.DMA((len(pieces),)),
        ],
        compiler_params=pltpu.CompilerParams(vmem_limit_bytes=58 << 20),
        name="expert",
    )(me, *pieces, w_gate, w_up, w_down)


def can_square(tokens, hidden):
    ep_size = lax.axis_size("ep")
    total = tokens * ep_size * lax.axis_size("dp")
    return lax.axis_size("dp") == 2 and ep_size % 4 == 0 and total <= 512 and hidden % 256 == 0


def experts_square(moe_input, expert_ids, gate_weights, w_gate, w_up, w_down):
    ep_size = lax.axis_size("ep")
    outer = ep_size // 4
    tokens, _ = moe_input.shape
    experts = jnp.arange(ep_size, dtype=jnp.int32)
    named = expert_ids[:, :, None] == experts[None, None, :]
    dense = jnp.sum(jnp.where(named, gate_weights[:, :, None], 0.0), axis=1)
    extra = split_exact(dense)
    lanes = -(-extra.shape[1] // 128) * 128
    extra = jnp.pad(extra, ((0, 0), (0, lanes - extra.shape[1])))
    rows = jnp.concatenate([moe_input, extra], axis=1)
    far = []
    for shift in range(1, outer):
        far.append(pull(rows, "ep", 4, outer, shift))
    own = jnp.concatenate([rows] + far, axis=0)
    by_x = pull(own, "dp", 1, 2, 1)
    by_y = pull(own, "ep", 2, 2, 1)
    both = pull(by_y, "dp", 1, 2, 1)
    near = [own, by_x, by_y, both]
    across = []
    for piece in near:
        across.append(pull(piece, "ep", 1, 2, 1))
    block = own.shape[0]
    places = [(n * block, 0) for n in range(8)]
    me = lax.axis_index("ep").astype(jnp.int32).reshape(1)
    keep, send = expert_call(
        me, near + across, tuple(places), 8 * block, ep_size, w_gate[0], w_up[0], w_down[0]
    )
    got = pull(send, "ep", 1, 2, 1)

    def part(n):
        rows = slice(n * block, (n + 1) * block)
        return keep[rows] + got[rows].astype(jnp.float32)

    got_both = pull(part(3).astype(jnp.bfloat16), "ep", 2, 2, 1)
    got_y = pull(part(2).astype(jnp.bfloat16), "ep", 2, 2, 1)
    yield None
    by_x = part(1) + got_both.astype(jnp.float32)
    got_x = pull(by_x.astype(jnp.bfloat16), "dp", 1, 2, 1)
    yield None
    own = part(0) + got_x.astype(jnp.float32) + got_y.astype(jnp.float32)
    near = []
    for shift in range(1, outer):
        piece = own[shift * tokens : (shift + 1) * tokens].astype(jnp.bfloat16)
        near.append(push(piece, "ep", 4, outer, shift))
    yield None
    total = own[:tokens]
    for piece in near:
        total = total + piece.astype(jnp.float32)
    yield total.astype(jnp.bfloat16)


def on_device(
    queries,
    suffix_latent,
    page_pool,
    page_owner,
    page_slot,
    prefix_len,
    moe_input,
    expert_ids,
    gate_weights,
    w_gate,
    w_up,
    w_down,
):
    packed, numbers = fetch_pages(page_pool, page_owner, page_slot)
    moe_args = (moe_input, expert_ids, gate_weights, w_gate, w_up, w_down)
    head_count = queries.shape[1] // KEY
    ranks = len(packed)

    def phase(rank, start, count, heads, before, so_far):
        return attend(
            queries,
            packed[rank],
            suffix_latent,
            numbers[rank],
            prefix_len,
            start,
            count,
            heads,
            before,
            rank == ranks - 1,
            so_far,
        )

    if ranks != 2 or not can_square(moe_input.shape[0], w_gate.shape[2]):
        moe_output = experts_staged(*moe_args)
        state = None
        for rank in range(ranks):
            state = phase(rank, 0, head_count, 2, state, None)
        return (state, moe_output)
    suffix_latent = lay_rows(*numbers, suffix_latent)
    stages = experts_square(*moe_args)
    heads = 4
    half = head_count // (2 * heads) * heads
    parts = [(0, half), (half, head_count - half)]
    next(stages)
    state = phase(0, 0, head_count, heads, None, None)
    attn_context = None
    for part in parts:
        next(stages)
        attn_context = phase(1, *part, heads, state, attn_context)
    moe_output = next(stages)
    return (attn_context, moe_output)


def solution(mesh):
    return jax.shard_map(
        on_device,
        mesh=mesh,
        in_specs=(
            P("ep", "dp"),
            P("ep", None),
            P("ep", None),
            P("ep", None),
            P("ep", None),
            P("ep"),
            P(("dp", "ep"), None),
            P(("dp", "ep"), None),
            P(("dp", "ep"), None),
            P("ep", None, "dp"),
            P("ep", None, "dp"),
            P("ep", "dp", None),
        ),
        out_specs=(P("ep", "dp"), P(("dp", "ep"), None)),
        check_vma=False,
    )
```

```python
import functools
import math

import jax
import jax.numpy as jnp
from jax import lax
from jax.experimental import pallas as pl
from jax.experimental.pallas import tpu as pltpu
from jax.sharding import PartitionSpec as P


LATENT = 512
ROPE = 64
KEY = LATENT + ROPE
PAGE = 64
LANES = 128

score_scale = 0.07216878364870322
neg_large = -1e30


def partner(pos, shift, size):
    return pos ^ shift if size & (size - 1) == 0 else (pos + shift) % size


def pull(values, axis, stride, size, shift, back=False):
    total = lax.axis_size(axis)
    pairs = []
    for dst in range(total):
        pos = (dst // stride) % size
        src = dst + (partner(pos, shift, size) - pos) * stride
        pairs.append((dst, src) if back else (src, dst))
    return lax.ppermute(values, axis, pairs)


def push(values, axis, stride, size, shift):
    return pull(values, axis, stride, size, shift, back=True)


def gather_stages():
    ep_size = lax.axis_size("ep")
    inner = 2 if ep_size % 2 == 0 else 1
    middle = 2 if ep_size % (2 * inner) == 0 else 1
    outer = ep_size // (inner * middle)
    stages = [
        ("ep", inner * middle, outer),
        ("dp", 1, lax.axis_size("dp")),
        ("ep", inner, middle),
        ("ep", 1, inner),
    ]
    return [stage for stage in stages if stage[2] > 1]


def attention_body(*refs, heads, together, tail, begins, ends, aliased):
    number_ref, length_ref, q_ref, packed_ref, *refs = refs
    if tail:
        suffix_ref, *refs = refs
    if not begins:
        acc_in_ref, state_in_ref, *refs = refs
    refs = refs[aliased:]
    if ends:
        o_ref, *refs = refs
    else:
        acc_ref, state_ref, *refs = refs
    k_ref, rotary_ref, bias_ref, sem = refs
    tokens = q_ref.shape[0]
    steps = rotary_ref.shape[0]
    prefix = steps * PAGE
    slabs = LATENT // LANES
    factor = score_scale * math.log2(math.e)

    @pl.when(pl.program_id(0) == 0)
    def load_keys():
        copies = []
        for t in range(slabs):
            copies.append(
                pltpu.make_async_copy(
                    packed_ref.at[:, pl.ds(t * PAGE, PAGE)],
                    k_ref.at[pl.ds(0, steps), :, pl.ds(t * LANES, LANES)],
                    sem.at[t],
                )
            )
        last = packed_ref.at[:, pl.ds(slabs * PAGE, PAGE // 2)]
        copies.append(pltpu.make_async_copy(last, rotary_ref, sem.at[slabs]))
        if tail:
            for n in range(tail // PAGE):
                copies.append(
                    pltpu.make_async_copy(
                        suffix_ref.at[pl.ds(n * PAGE, PAGE)],
                        k_ref.at[steps + n],
                        sem.at[slabs + 1 + n],
                    )
                )
        for copy in copies:
            copy.start()
        lane = lax.broadcasted_iota(jnp.int32, (1, 2 * PAGE), 1)
        for pair in range(steps // 2):
            low = number_ref[2 * pair] * PAGE
            high = number_ref[2 * pair + 1] * PAGE - PAGE
            position = lane + jnp.where(lane < PAGE, low, high)
            seen = jnp.where(position < length_ref[0], 0.0, neg_large)
            bias_ref[:, 2 * PAGE * pair : 2 * PAGE * (pair + 1)] = seen.astype(jnp.float32)
        for copy in copies:
            copy.wait()
        half = PAGE // 2
        for n in range(steps):
            both = rotary_ref[n]
            k_ref[n, :half, LATENT:] = both[:, :ROPE]
            k_ref[n, half:, LATENT:] = both[:, ROPE:]

    bias = bias_ref[...]
    keys = k_ref[...].reshape(prefix + tail, KEY)
    if tail:
        row = lax.broadcasted_iota(jnp.int32, (tokens, tail), 0)
        col = lax.broadcasted_iota(jnp.int32, (tokens, tail), 1)
        causal = jnp.where(col <= row, 0.0, neg_large).astype(jnp.float32)
        causal = jnp.concatenate([causal] * together, axis=0)
    for first in range(0, heads, together):
        group = range(first, first + together)
        q = jnp.concatenate([q_ref[:, h * KEY : (h + 1) * KEY] for h in group], axis=0)
        s = lax.dot_general(
            q, keys, (((1,), (1,)), ((), ())), preferred_element_type=jnp.float32
        )
        blocks = [s[:, :prefix] + bias]
        if tail:
            blocks.append(s[:, prefix:] + causal)
        tops = [jnp.max(block, axis=1, keepdims=True) for block in blocks]
        if not begins:
            states = [state_in_ref[:, h * LANES : (h + 1) * LANES] for h in group]
            state = jnp.concatenate(states, axis=0)
            before = state[:, :1]
            tops.append(before)
        m = functools.reduce(jnp.maximum, tops)
        shift = m * factor
        powers = [jnp.exp2(block * factor - shift) for block in blocks]
        total = sum(jnp.sum(power, axis=1, keepdims=True) for power in powers)
        p = jnp.concatenate([power.astype(jnp.bfloat16) for power in powers], axis=1)
        acc = jnp.dot(p, keys[:, :LATENT], preferred_element_type=jnp.float32)
        if not begins:
            scale = jnp.exp2(before * factor - shift)
            total = total + state[:, LANES - 1 :] * scale
            olds = [acc_in_ref[:, h * LATENT : (h + 1) * LATENT] for h in group]
            acc = acc + jnp.concatenate(olds, axis=0) * scale
        if ends:
            acc = acc * (1.0 / total)
        else:
            lane = lax.broadcasted_iota(jnp.int32, (acc.shape[0], LANES), 1)
            state = jnp.where(lane < LANES // 2, m, total)
        for n, h in enumerate(group):
            rows = slice(n * tokens, (n + 1) * tokens)
            if ends:
                o_ref[:, h * LATENT : (h + 1) * LATENT] = acc[rows].astype(jnp.bfloat16)
            else:
                acc_ref[:, h * LATENT : (h + 1) * LATENT] = acc[rows]
                state_ref[:, h * LANES : (h + 1) * LANES] = state[rows]


def attend(
    queries, packed, suffix, numbers, length, start, count, heads, before=None, ends=True, so_far=None
):
    tokens = queries.shape[0]
    head_count = queries.shape[1] // KEY
    steps = packed.shape[0]
    prefix = steps * PAGE
    begins = before is None
    tail = suffix.shape[0] if begins else 0
    together = 4 if heads % 4 == 0 and prefix <= 2048 else 2
    offset = start // heads
    aliased = 0 if so_far is None else 1
    scalars = pl.BlockSpec(memory_space=pltpu.SMEM)
    anywhere = pl.BlockSpec(memory_space=pl.ANY)
    operands = [numbers, length, queries, packed]
    in_specs = [
        scalars,
        scalars,
        pl.BlockSpec((tokens, heads * KEY), lambda i: (0, i + offset)),
        anywhere,
    ]
    if begins:
        operands.append(suffix)
        in_specs.append(anywhere)
    else:
        operands += before
        in_specs += [
            pl.BlockSpec((tokens, heads * LATENT), lambda i: (0, i + offset)),
            pl.BlockSpec((tokens, heads * LANES), lambda i: (0, i + offset)),
        ]
    if aliased:
        operands.append(so_far)
        in_specs.append(anywhere)
    if ends:
        out_specs = pl.BlockSpec((tokens, heads * LATENT), lambda i: (0, i + offset))
        out_shape = jax.ShapeDtypeStruct((tokens, head_count * LATENT), jnp.bfloat16)
    else:
        out_specs = [
            pl.BlockSpec((tokens, heads * LATENT), lambda i: (0, i)),
            pl.BlockSpec((tokens, heads * LANES), lambda i: (0, i)),
        ]
        out_shape = [
            jax.ShapeDtypeStruct((tokens, count * LATENT), jnp.float32),
            jax.ShapeDtypeStruct((tokens, count * LANES), jnp.float32),
        ]
    return pl.pallas_call(
        functools.partial(
            attention_body,
            heads=heads,
            together=together,
            tail=tail,
            begins=begins,
            ends=ends,
            aliased=aliased,
        ),
        grid=(count // heads,),
        in_specs=in_specs,
        out_specs=out_specs,
        out_shape=out_shape,
        scratch_shapes=[
            pltpu.VMEM((steps + tail // PAGE, PAGE, KEY), jnp.bfloat16),
            pltpu.VMEM((steps, PAGE // 2, LANES), jnp.bfloat16),
            pltpu.VMEM((1, prefix), jnp.float32),
            pltpu.SemaphoreType.DMA((LATENT // LANES + 1 + tail // PAGE,)),
        ],
        input_output_aliases={len(operands) - 1: 0} if aliased else {},
        compiler_params=pltpu.CompilerParams(vmem_limit_bytes=58 << 20),
        name="attend",
    )(*operands)


def lay_body(first_ref, second_ref, rows_ref, out_ref):
    out_ref[...] = rows_ref[...]


def lay_rows(first, second, rows):
    scalars = pl.BlockSpec(memory_space=pltpu.SMEM)
    whole = pl.BlockSpec(memory_space=pltpu.VMEM)
    return pl.pallas_call(
        lay_body,
        in_specs=[scalars, scalars, whole],
        out_specs=whole,
        out_shape=jax.ShapeDtypeStruct(rows.shape, rows.dtype),
        name="lay",
    )(first, second, rows)


def fetch_pages(page_pool, page_owner, page_slot):
    ep_size = lax.axis_size("ep")
    pages = page_owner.shape[1]
    ranks = (pages + ep_size - 1) // ep_size
    page_id = jnp.arange(pages, dtype=jnp.int32)
    owners = jnp.arange(ep_size, dtype=jnp.int32)
    rank_id = jnp.arange(ranks, dtype=jnp.int32)
    match = (page_owner[0][None, None, :] == owners[:, None, None]) & (
        page_id[None, None, :] // ep_size == rank_id[None, :, None]
    )
    wanted = jnp.sum(jnp.where(match, page_slot[0][None, None, :], 0), axis=2)
    asked = lax.all_to_all(wanted, "ep", split_axis=0, concat_axis=0, tiled=True)
    pool = page_pool.reshape(page_pool.shape[0], PAGE, KEY)
    place = jnp.arange(ep_size, dtype=jnp.int32)

    def number(first):
        low = first * ep_size
        ids = low + jnp.arange(min(ep_size, pages), dtype=jnp.int32)
        held = lax.dynamic_slice_in_dim(page_owner[0], low, min(ep_size, pages))
        hit = place[:, None] == held[None, :]
        return pages + jnp.sum(jnp.where(hit, ids[None, :] - pages, 0), axis=1)

    dp_size = lax.axis_size("dp")
    if ranks == dp_size and pages == ranks * ep_size:
        plane = lax.axis_index("dp").astype(jnp.int32)
        chosen = pick_pages(plane.reshape(1), asked, pool)
        own = lax.all_to_all(chosen, "ep", split_axis=0, concat_axis=0, tiled=True)
        fetched, numbers = [own], [number(plane)]
        for shift in range(1, dp_size):
            fetched.append(pull(own, "dp", 1, dp_size, shift))
            numbers.append(number(partner(plane, jnp.int32(shift), dp_size)))
        return fetched, numbers
    fetched, numbers = [], []
    for r in range(ranks):
        chosen = pick_pages(jnp.full((1,), r, jnp.int32), asked, pool)
        fetched.append(lax.all_to_all(chosen, "ep", split_axis=0, concat_axis=0, tiled=True))
        numbers.append(number(jnp.int32(r)))
    return fetched, numbers


def pick_body(rank_ref, asked_ref, pool_ref, out_ref):
    slabs = LATENT // LANES
    half = PAGE // 2
    for n in range(asked_ref.shape[0]):
        page = pool_ref[asked_ref[n, rank_ref[0]]]
        for t in range(slabs):
            out_ref[n, t * PAGE : (t + 1) * PAGE] = page[:, t * LANES : (t + 1) * LANES]
        rotary = page[:, LATENT:]
        out_ref[n, slabs * PAGE :] = jnp.concatenate([rotary[:half], rotary[half:]], axis=1)


def pick_pages(rank, asked, pool):
    scalars = pl.BlockSpec(memory_space=pltpu.SMEM)
    whole = pl.BlockSpec(memory_space=pltpu.VMEM)
    shape = (asked.shape[0], PAGE * KEY // LANES, LANES)
    return pl.pallas_call(
        pick_body,
        in_specs=[scalars, scalars, whole],
        out_specs=whole,
        out_shape=jax.ShapeDtypeStruct(shape, pool.dtype),
        name="pick",
    )(rank, asked, pool)


def split_exact(values):
    high = values.astype(jnp.bfloat16)
    rest = values - high.astype(jnp.float32)
    mid = rest.astype(jnp.bfloat16)
    low = (rest - mid.astype(jnp.float32)).astype(jnp.bfloat16)
    return jnp.concatenate([high, mid, low], axis=1)


def experts_staged(moe_input, expert_ids, gate_weights, w_gate, w_up, w_down):
    ep_size = lax.axis_size("ep")
    _, features = moe_input.shape
    experts = jnp.arange(ep_size, dtype=jnp.int32)
    named = expert_ids[:, :, None] == experts[None, None, :]
    dense = jnp.sum(jnp.where(named, gate_weights[:, :, None], 0.0), axis=1)
    extra = split_exact(dense)
    lanes = -(-extra.shape[1] // 128) * 128
    extra = jnp.pad(extra, ((0, 0), (0, lanes - extra.shape[1])))
    rows = jnp.concatenate([moe_input, extra], axis=1)
    stages = gather_stages()
    for axis, stride, size in stages:
        rows = jnp.concatenate(
            [rows] + [pull(rows, axis, stride, size, shift) for shift in range(1, size)], axis=0
        )
    inputs = rows[:, :features]
    parts = rows[:, features : features + 3 * ep_size].astype(jnp.float32)
    parts = parts.reshape(-1, 3, ep_size)
    here = (experts == lax.axis_index("ep"))[None, None, :]
    parts = jnp.sum(jnp.where(here, parts, 0.0), axis=2)
    weight = (parts[:, 0] + parts[:, 1] + parts[:, 2])[:, None]
    gate_proj = jnp.dot(inputs, w_gate[0], preferred_element_type=jnp.float32)
    up_proj = jnp.dot(inputs, w_up[0], preferred_element_type=jnp.float32)
    hidden = (jax.nn.silu(gate_proj) * up_proj).astype(jnp.bfloat16)
    kept = jnp.dot(hidden, w_down[0], preferred_element_type=jnp.float32) * weight
    for axis, stride, size in reversed(stages):
        count = kept.shape[0] // size
        moved = [
            push(kept[s * count : (s + 1) * count].astype(jnp.bfloat16), axis, stride, size, s)
            for s in range(1, size)
        ]
        kept = kept[:count]
        for m in moved:
            kept = kept + m.astype(jnp.float32)
    return kept.astype(jnp.bfloat16)


def expert_body(me_ref, *refs, places, hidden_steps, experts, features):
    pieces = refs[: len(places)]
    gate_ref, up_ref, down_ref, keep_ref, send_ref, far_ref, *refs = refs[len(places) :]
    x_ref, h_ref, w_ref, sem = refs
    step = pl.program_id(0)

    @pl.when(step == 0)
    def load_rows():
        copies = []
        for n, (piece, (row, lane)) in enumerate(zip(pieces, places, strict=True)):
            rows, lanes = piece.shape
            copies.append(
                pltpu.make_async_copy(
                    piece, x_ref.at[pl.ds(row, rows), pl.ds(lane, lanes)], sem.at[n]
                )
            )
        for copy in copies:
            copy.start()
        for copy in copies:
            copy.wait()
        tags = x_ref[:, features:].astype(jnp.float32)
        lane = lax.broadcasted_iota(jnp.int32, tags.shape, 1)
        mine = (lane % experts == me_ref[0]) & (lane < 3 * experts)
        w_ref[...] = jnp.sum(jnp.where(mine, tags, 0.0), axis=1, keepdims=True)

    block = gate_ref.shape[1]
    for n in range(hidden_steps):

        @pl.when(step == n)
        def first_layer(n=n):
            x = x_ref[:, :features]
            gate = jnp.dot(x, gate_ref[...], preferred_element_type=jnp.float32)
            up = jnp.dot(x, up_ref[...], preferred_element_type=jnp.float32)
            hidden = gate / (1.0 + jnp.exp(-gate)) * up
            h_ref[:, n * block : (n + 1) * block] = hidden.astype(jnp.bfloat16)

    @pl.when(step >= hidden_steps)
    def second_layer():
        part = jnp.dot(h_ref[...], down_ref[...], preferred_element_type=jnp.float32)
        total = part * w_ref[...]
        half = keep_ref.shape[0]
        keep_ref[...] = total[:half]
        near = half + send_ref.shape[0]
        send_ref[...] = total[half:near].astype(jnp.bfloat16)
        far_ref[...] = total[near:].astype(jnp.bfloat16)


def expert_call(me, pieces, places, rows, experts, w_gate, w_up, w_down):
    features, hidden = w_gate.shape
    width = pieces[0].shape[1]
    block = 256
    wide = features // 2 if features % 512 == 0 else 128
    steps = hidden // block
    anywhere = pl.BlockSpec(memory_space=pl.ANY)
    heights = (rows // 2, 3 * rows // 8, rows // 8)
    outs = [pl.BlockSpec((n, wide), lambda i: (0, jnp.maximum(i - steps, 0))) for n in heights]
    return pl.pallas_call(
        functools.partial(
            expert_body, places=places, hidden_steps=steps, experts=experts, features=features
        ),
        grid=(steps + features // wide,),
        in_specs=[
            pl.BlockSpec(memory_space=pltpu.SMEM),
            *[anywhere] * len(pieces),
            pl.BlockSpec((features, block), lambda i: (0, jnp.minimum(i, steps - 1))),
            pl.BlockSpec((features, block), lambda i: (0, jnp.minimum(i, steps - 1))),
            pl.BlockSpec((hidden, wide), lambda i: (0, jnp.maximum(i - steps, 0))),
        ],
        out_specs=outs,
        out_shape=[
            jax.ShapeDtypeStruct((heights[0], features), jnp.float32),
            jax.ShapeDtypeStruct((heights[1], features), jnp.bfloat16),
            jax.ShapeDtypeStruct((heights[2], features), jnp.bfloat16),
        ],
        scratch_shapes=[
            pltpu.VMEM((rows, width), jnp.bfloat16),
            pltpu.VMEM((rows, hidden), jnp.bfloat16),
            pltpu.VMEM((rows, 1), jnp.float32),
            pltpu.SemaphoreType.DMA((len(pieces),)),
        ],
        compiler_params=pltpu.CompilerParams(vmem_limit_bytes=58 << 20),
        name="expert",
    )(me, *pieces, w_gate, w_up, w_down)


def can_square(tokens, hidden):
    ep_size = lax.axis_size("ep")
    total = tokens * ep_size * lax.axis_size("dp")
    return lax.axis_size("dp") == 2 and ep_size % 4 == 0 and total <= 512 and hidden % 256 == 0


def experts_square(moe_input, expert_ids, gate_weights, w_gate, w_up, w_down):
    ep_size = lax.axis_size("ep")
    outer = ep_size // 4
    tokens, _ = moe_input.shape
    experts = jnp.arange(ep_size, dtype=jnp.int32)
    named = expert_ids.T[None, :, :] == experts[:, None, None]
    dense = jnp.sum(jnp.where(named, gate_weights.T[None, :, :], 0.0), axis=1).T
    extra = split_exact(dense)
    lanes = -(-extra.shape[1] // 128) * 128
    extra = jnp.pad(extra, ((0, 0), (0, lanes - extra.shape[1])))
    rows = jnp.concatenate([moe_input, extra], axis=1)
    far = []
    for shift in range(1, outer):
        far.append(pull(rows, "ep", 4, outer, shift))
    own = jnp.concatenate([rows] + far, axis=0)
    by_x = pull(own, "dp", 1, 2, 1)
    by_y = pull(own, "ep", 2, 2, 1)
    both = pull(by_y, "dp", 1, 2, 1)
    near = [own, by_x, by_y, both]
    across = []
    for piece in near:
        across.append(pull(piece, "ep", 1, 2, 1))
    block = own.shape[0]
    places = [(n * block, 0) for n in range(8)]
    me = lax.axis_index("ep").astype(jnp.int32).reshape(1)
    keep, send, send_far = expert_call(
        me, near + across, tuple(places), 8 * block, ep_size, w_gate[0], w_up[0], w_down[0]
    )
    got_far = pull(send_far, "ep", 1, 2, 1)
    got = pull(send, "ep", 1, 2, 1)

    def part(n):
        rows = slice(n * block, (n + 1) * block)
        other = got_far if n == 3 else got[rows]
        return keep[rows] + other.astype(jnp.float32)

    got_both = pull(part(3).astype(jnp.bfloat16), "ep", 2, 2, 1)
    got_y = pull(part(2).astype(jnp.bfloat16), "ep", 2, 2, 1)
    yield None
    by_x = part(1) + got_both.astype(jnp.float32)
    got_x = pull(by_x.astype(jnp.bfloat16), "dp", 1, 2, 1)
    yield None
    own = part(0) + got_x.astype(jnp.float32) + got_y.astype(jnp.float32)
    near = []
    for shift in range(1, outer):
        piece = own[shift * tokens : (shift + 1) * tokens].astype(jnp.bfloat16)
        near.append(push(piece, "ep", 4, outer, shift))
    yield None
    total = own[:tokens]
    for piece in near:
        total = total + piece.astype(jnp.float32)
    yield total.astype(jnp.bfloat16)


def on_device(
    queries,
    suffix_latent,
    page_pool,
    page_owner,
    page_slot,
    prefix_len,
    moe_input,
    expert_ids,
    gate_weights,
    w_gate,
    w_up,
    w_down,
):
    packed, numbers = fetch_pages(page_pool, page_owner, page_slot)
    moe_args = (moe_input, expert_ids, gate_weights, w_gate, w_up, w_down)
    head_count = queries.shape[1] // KEY
    ranks = len(packed)

    def phase(rank, start, count, heads, before, so_far):
        return attend(
            queries,
            packed[rank],
            suffix_latent,
            numbers[rank],
            prefix_len,
            start,
            count,
            heads,
            before,
            rank == ranks - 1,
            so_far,
        )

    if ranks != 2 or not can_square(moe_input.shape[0], w_gate.shape[2]):
        moe_output = experts_staged(*moe_args)
        state = None
        for rank in range(ranks):
            state = phase(rank, 0, head_count, 2, state, None)
        return (state, moe_output)
    suffix_latent = lay_rows(*numbers, suffix_latent)
    stages = experts_square(*moe_args)
    heads = 4
    half = head_count // (2 * heads) * heads
    parts = [(0, half), (half, head_count - half)]
    next(stages)
    state = phase(0, 0, head_count, heads, None, None)
    attn_context = None
    for part in parts:
        next(stages)
        attn_context = phase(1, *part, heads, state, attn_context)
    moe_output = next(stages)
    return (attn_context, moe_output)


def solution(mesh):
    return jax.shard_map(
        on_device,
        mesh=mesh,
        in_specs=(
            P("ep", "dp"),
            P("ep", None),
            P("ep", None),
            P("ep", None),
            P("ep", None),
            P("ep"),
            P(("dp", "ep"), None),
            P(("dp", "ep"), None),
            P(("dp", "ep"), None),
            P("ep", None, "dp"),
            P("ep", None, "dp"),
            P("ep", "dp", None),
        ),
        out_specs=(P("ep", "dp"), P(("dp", "ep"), None)),
        check_vma=False,
    )
```
